32 devices in a mesh: tm: 8 (over z, y), lm: 4 (over x, core).
Axes of the slice: x: 2, y: 2, z: 4, core: 2. Of those that a mesh axis runs over, the one named last changes fastest.
Arguments:
- knot_right_side: float32 [6, 128, 128], P(None, 'tm')
- land_rhs: float32 [3, 131072], P(None, ('tm', 'lm'))
- jac_knot: bfloat16 [3072, 32, 384], P(('tm', 'lm')), may hold values from -0.21875 to 0.21875
- jac_land: bfloat16 [3072, 32, 192], P(('tm', 'lm')), may hold values from -0.5 to 0.5
- obs_knot: int32 [3072], P(('tm', 'lm')), may hold values from 0 to 31
- obs_slot: int32 [3072], P(('tm', 'lm')), may hold values from 0 to 127
- obs_count: int32 [3072], P(('tm', 'lm')), may hold values from 8 to 32
- send_list: int32 [32, 32, 4], P(('tm', 'lm')), may hold values from 0 to 63
- couple: float32 [6, 6, 128, 128], P(None, None, 'tm')
- knot_dinv: float32 [6, 6, 128, 128], P(None, None, 'tm')
- cuts: int32 [128, 128], P('tm'), may hold values 0 or 1
- land_pinv: float32 [3, 3, 131072], P(None, None, ('tm', 'lm'))
- knot_damp: float32 [6, 128, 128], P(None, 'tm'), may hold values from 0.3 to 3
- land_damp: float32 [3, 131072], P(None, ('tm', 'lm')), may hold values from 0.3 to 3
Outputs:
- knot_step: float32 [6, 128, 128], P(None, 'tm')
- land_step: float32 [3, 131072], P(None, ('tm', 'lm'))
- knot_resid: float32 [6, 128, 128], P(None, 'tm')
- land_resid: float32 [3, 131072], P(None, ('tm', 'lm'))
The draws below stay inside these ranges and needn't reach their ends.
Inputs may be any that keep to these rules, and one draw needn't show every extreme that they name: send_list[s, d, c] is the local landmark block of device s that device s places into its slot c for device d; blocks may repeat. Observation block o sees the landmark block that device obs_slot[o] // 4 places into slot obs_slot[o] % 4 for device o // 96. obs_knot[o] = j names the knot block of vehicles 4 * j to 4 * j + 3 on the time index o // 384.
All inputs are finite; a program needn't handle non-finite values. No bound on the sum of `cuts` on one device may be relied on, other than what follows from the above.
Results may differ from the reference program's by a relative error of at most 0.00115.
Values may be sent and summed in bfloat16 or wider, within the bound.
No kernel may reach another device: no remote copies, remote signals or barrier semaphores. Data moves between devices by JAX's collectives and lax.ppermute only.
A program may use at most 192 MiB of HBM per device.

```python
import math
import jax
import jax.numpy as jnp
from jax import lax

VEHICLE_TOTAL = 128
VB = 4
K_DEV = 16
LB = 64
LB_DEV = 64
R = 32
B_DEV = 96
ITERS = 3
SPLINE_POINTS = 128
KB_DEV = 32
KW = 384
LW = 192
SENDERS = 32
NLB = 2048
NL = 131072
NOB = 3072
CAP = 4
SLOTS = 128
N_TM = 8
N_LM = 4


def draw_couple(key, part):
    seeded_generators = jax.random.split(jax.random.fold_in(key, 11), 5)
    lengths = jnp.exp(jax.random.uniform(seeded_generators[0], (6, 1, VEHICLE_TOTAL), minval=math.log(20.0), maxval=math.log(4.0 * SPLINE_POINTS)))
    jitter = jax.random.uniform(seeded_generators[1], (6, SPLINE_POINTS, VEHICLE_TOTAL), minval=0.5, maxval=2.0)
    frequency_levels = jnp.exp(-jitter / lengths)
    clustered_batches = jax.random.uniform(seeded_generators[2], (1, SPLINE_POINTS, VEHICLE_TOTAL)) < 3.0 / SPLINE_POINTS
    magnitude_multiplier = jax.random.uniform(seeded_generators[3], (1, SPLINE_POINTS, VEHICLE_TOTAL), minval=0.5, maxval=0.8)
    frequency_levels = jnp.where(clustered_batches, frequency_levels * magnitude_multiplier, frequency_levels)
    skew = jax.random.normal(seeded_generators[4], (SPLINE_POINTS, VEHICLE_TOTAL, 6, 6)) * 0.35
    skew = skew - jnp.swapaxes(skew, -1, -2)
    unit = jnp.broadcast_to(jnp.eye(6, dtype=jnp.float32), (SPLINE_POINTS, VEHICLE_TOTAL, 6, 6))
    rotation = jnp.linalg.solve(unit - skew, unit + skew)
    rotation = jnp.transpose(rotation, (2, 3, 0, 1))
    return (frequency_levels[:, None, :, :] * rotation).astype(jnp.float32)


def draw_knot_dinv(key, part):
    seeded_generators = jax.random.split(jax.random.fold_in(key, 23), 2)
    base = jax.random.normal(seeded_generators[0], (SPLINE_POINTS, VEHICLE_TOTAL, 6, 6))
    inner = jnp.einsum('kvab,kvcb->kvac', base, base) / 6.0 + 0.6 * jnp.eye(6, dtype=jnp.float32)
    scale = 4.0 / math.sqrt(SPLINE_POINTS) * jnp.exp(jax.random.uniform(seeded_generators[1], (SPLINE_POINTS, VEHICLE_TOTAL), minval=0.0, maxval=math.log(4.0)))
    return jnp.transpose(inner * scale[:, :, None, None], (2, 3, 0, 1)).astype(jnp.float32)


def draw_land_pinv(key, part):
    seeded_generators = jax.random.split(jax.random.fold_in(key, 37), 2)
    base = jax.random.normal(seeded_generators[0], (NL, 3, 3))
    inner = jnp.einsum('nab,ncb->nac', base, base) / 3.0 + 0.5 * jnp.eye(3, dtype=jnp.float32)
    scale = jnp.exp(jax.random.uniform(seeded_generators[1], (NL,), minval=math.log(0.3), maxval=math.log(1.5)))
    return jnp.transpose(inner * scale[:, None, None], (1, 2, 0)).astype(jnp.float32)


def draw_knot_right_side(key, part):
    seeded_generators = jax.random.split(jax.random.fold_in(key, 41), 3)
    position = jnp.arange(SPLINE_POINTS, dtype=jnp.float32) / (SPLINE_POINTS - 1)
    ramp = (1.0 + 2.0 * position)[None, :, None]
    vehicle_scale = jnp.exp(jax.random.uniform(seeded_generators[0], (1, 1, VEHICLE_TOTAL), minval=math.log(0.3), maxval=math.log(3.0)))
    channel_scale = jnp.exp(jax.random.uniform(seeded_generators[1], (6, 1, 1), minval=0.0, maxval=math.log(3.0)))
    values = jax.random.normal(seeded_generators[2], (6, SPLINE_POINTS, VEHICLE_TOTAL)) * ramp
    return (values * vehicle_scale * channel_scale).astype(jnp.float32)


def draw_land_rhs(key, part):
    seeded_generators = jax.random.split(jax.random.fold_in(key, 53), 3)
    position = jnp.arange(NL, dtype=jnp.float32) / (NL - 1)
    ramp = (1.0 + 2.0 * position)[None, :]
    landmark_spread = jnp.exp(jax.random.uniform(seeded_generators[0], (1, NL), minval=math.log(0.3), maxval=math.log(3.0)))
    channel_scale = jnp.exp(jax.random.uniform(seeded_generators[1], (3, 1), minval=0.0, maxval=math.log(3.0)))
    values = jax.random.normal(seeded_generators[2], (3, NL)) * ramp
    return (values * landmark_spread * channel_scale).astype(jnp.float32)


def place_ends(entries, key, least, high):
    longest = entries.shape.index(max(entries.shape))
    spots = []
    for shift in (0, 1):
        where = [jax.random.randint(jax.random.fold_in(key, axis), (), 0, length) for axis, length in enumerate(entries.shape)]
        where[longest] = (where[longest] + shift) % entries.shape[longest]
        spots.append(tuple(where))
    return entries.at[spots[0]].set(least).at[spots[1]].set(high)


def levels(rng, shape, cuts, least, high):
    gain = 1.0
    for dim, shards_of in cuts:
        heights = jax.random.uniform(jax.random.fold_in(jax.random.fold_in(rng, 6), dim), (shards_of,), jnp.float32, least / len(cuts), high / len(cuts))
        gain = gain * jnp.repeat(jnp.exp(heights), shape[dim] // shards_of).reshape((-1,) + (1,) * (len(shape) - 1 - dim))
    return gain


def centred(own_key, dims, width, limit, pieces=(), kind=jnp.bfloat16):
    values = jax.random.normal(own_key, dims, jnp.float32) * width
    if len(pieces) > 0:
        values = levels(own_key, dims, pieces, -0.22, 0.18) * values
    return jnp.clip(values, min=-limit, max=limit).astype(kind)


def setup_inputs(seed: int = 0) -> dict:
    streams_of = jax.random.split(jax.random.key(seed), 15)
    knot_right_side = draw_knot_right_side(jax.random.fold_in(streams_of[14], 71), 0)
    land_rhs = draw_land_rhs(jax.random.fold_in(streams_of[14], 71), 0)
    jac_knot = centred(streams_of[2], (NOB, R, KW), (R * 24) ** -0.5, 0.21875, ((0, 32),))
    jac_land = centred(streams_of[3], (NOB, R, LW), (R * 4) ** -0.5, 0.5, ((0, 32),))
    obs_knot = place_ends(jax.random.randint(streams_of[4], (NOB,), 0, KB_DEV), jax.random.fold_in(streams_of[4], 1), 0, KB_DEV - 1).astype(jnp.int32)
    obs_slot = place_ends(jax.random.randint(streams_of[5], (NOB,), 0, SLOTS), jax.random.fold_in(streams_of[5], 1), 0, SLOTS - 1).astype(jnp.int32)
    obs_count = place_ends(jax.random.randint(streams_of[6], (NOB,), R // 4, R + 1), jax.random.fold_in(streams_of[6], 1), R // 4, R).astype(jnp.int32)
    send_list = place_ends(jax.random.randint(streams_of[7], (SENDERS, SENDERS, CAP), 0, LB_DEV), jax.random.fold_in(streams_of[7], 1), 0, LB_DEV - 1).astype(jnp.int32)
    couple = draw_couple(jax.random.fold_in(streams_of[14], 71), 0)
    knot_dinv = draw_knot_dinv(jax.random.fold_in(streams_of[14], 71), 0)
    cuts = place_ends((jax.random.randint(streams_of[10], (SPLINE_POINTS, VEHICLE_TOTAL), 0, 4 * SPLINE_POINTS) < 1).astype(jnp.int32), jax.random.fold_in(streams_of[10], 1), 0, 1)
    land_pinv = draw_land_pinv(jax.random.fold_in(streams_of[14], 71), 0)
    knot_damp = jnp.clip(jnp.exp(math.log(3.0) - 2.3025851 * jax.random.uniform(streams_of[12], (6, SPLINE_POINTS, VEHICLE_TOTAL), jnp.float32) ** levels(streams_of[12], (6, SPLINE_POINTS, VEHICLE_TOTAL), ((1, 8),), -0.2, 0.2)), 0.3, 3.0)
    land_damp = jnp.clip(jnp.exp(math.log(3.0) - 2.3025851 * jax.random.uniform(streams_of[13], (3, NL), jnp.float32) ** levels(streams_of[13], (3, NL), ((1, 32),), -0.2, 0.2)), 0.3, 3.0)
    return {"knot_right_side": knot_right_side, "land_rhs": land_rhs, "jac_knot": jac_knot, "jac_land": jac_land, "obs_knot": obs_knot, "obs_slot": obs_slot, "obs_count": obs_count, "send_list": send_list, "couple": couple, "knot_dinv": knot_dinv, "cuts": cuts, "land_pinv": land_pinv, "knot_damp": knot_damp, "land_damp": land_damp}


highest = lax.Precision.HIGHEST

def knot_blocks(field):
    shaped = field.reshape(6, N_TM, K_DEV, KB_DEV, VB)
    return jnp.transpose(shaped, (1, 3, 0, 2, 4)).reshape(N_TM * KB_DEV, KW)

def knot_field(blocks):
    shaped = blocks.reshape(N_TM, KB_DEV, 6, K_DEV, VB)
    return jnp.transpose(shaped, (2, 0, 3, 1, 4)).reshape(6, SPLINE_POINTS, VEHICLE_TOTAL)

def land_blocks(field):
    return jnp.transpose(field.reshape(3, NLB, LB), (1, 0, 2)).reshape(NLB, LW)

def land_field(blocks):
    return jnp.transpose(blocks.reshape(NLB, 3, LB), (1, 0, 2)).reshape(3, NL)

def hessian_product(knot_dir, land_dir, jac_knot, jac_land, obs_knot, obs_slot, obs_count, send_list, knot_damp, land_damp):
    knot_bf = knot_blocks(knot_dir.astype(jnp.bfloat16))
    land_bf = land_blocks(land_dir.astype(jnp.bfloat16))
    row_index = jnp.arange(R, dtype=jnp.int32)

    def per_unit_term(carry, device):
        knot_acc, land_acc = carry
        first = (device * B_DEV).astype(jnp.int32)
        jac_k = lax.dynamic_slice_in_dim(jac_knot, first, B_DEV, 0).astype(jnp.float32)
        jac_l = lax.dynamic_slice_in_dim(jac_land, first, B_DEV, 0).astype(jnp.float32)
        knots_here = lax.dynamic_slice_in_dim(obs_knot, first, B_DEV, 0)
        slots_here = lax.dynamic_slice_in_dim(obs_slot, first, B_DEV, 0)
        counts_here = lax.dynamic_slice_in_dim(obs_count, first, B_DEV, 0)
        knot_index = (device // N_LM * KB_DEV + knots_here).astype(jnp.int32)
        owner = slots_here // CAP
        column = slots_here % CAP
        land_index = (owner * LB_DEV + send_list[owner, device, column]).astype(jnp.int32)
        knot_in = knot_bf[knot_index].astype(jnp.float32)
        land_in = land_bf[land_index].astype(jnp.float32)
        resid = jnp.einsum('orc,oc->or', jac_k, knot_in, precision=highest) + jnp.einsum('orc,oc->or', jac_l, land_in, precision=highest)
        mask = (row_index[None, :] < counts_here[:, None]).astype(jnp.float32)
        resid_bf = (resid * mask).astype(jnp.bfloat16).astype(jnp.float32)
        knot_terms = jnp.einsum('orc,or->oc', jac_k, resid_bf, precision=highest)
        land_terms = jnp.einsum('orc,or->oc', jac_l, resid_bf, precision=highest)
        return ((knot_acc.at[knot_index].add(knot_terms), land_acc.at[land_index].add(land_terms)), None)
    start = (jnp.zeros((N_TM * KB_DEV, KW), jnp.float32), jnp.zeros((NLB, LW), jnp.float32))
    (knot_acc, land_acc), _ = lax.scan(per_unit_term, start, jnp.arange(N_TM * N_LM, dtype=jnp.int32))
    return (knot_field(knot_acc) + knot_damp * knot_dir, land_field(land_acc) + land_damp * land_dir)

def precondition(knot_res, land_res, couple, knot_dinv, cuts, land_pinv):
    live = couple * (1 - cuts).astype(jnp.float32)[None, None]
    chain = jnp.moveaxis(live, 2, 0)
    dinv_chain = jnp.moveaxis(knot_dinv, 2, 0)

    def advance(carry, item):
        value = item[1] + carry
        return (-jnp.einsum('abv,bv->av', item[0], value, precision=highest), value)
    _, wvalues = lax.scan(advance, jnp.zeros((6, VEHICLE_TOTAL), jnp.float32), (chain, jnp.moveaxis(knot_res, 1, 0)))
    scaled = jnp.einsum('kabv,kbv->kav', dinv_chain, wvalues, precision=highest)

    def retreat(carry, item):
        value = item[1] - jnp.einsum('bav,bv->av', item[0], carry, precision=highest)
        return (value, value)
    _, vvalues = lax.scan(retreat, jnp.zeros((6, VEHICLE_TOTAL), jnp.float32), (chain, scaled), reverse=True)
    land_z = jnp.einsum('abn,bn->an', land_pinv, land_res, precision=highest)
    return (jnp.moveaxis(vvalues, 0, 1), land_z)

def reference(knot_right_side, land_rhs, jac_knot, jac_land, obs_knot, obs_slot, obs_count, send_list, couple, knot_dinv, cuts, land_pinv, knot_damp, land_damp):
    knot_step = jnp.zeros_like(knot_right_side)
    land_step = jnp.zeros_like(land_rhs)
    knot_resid = knot_right_side
    land_resid = land_rhs
    knot_z, land_z = precondition(knot_resid, land_resid, couple, knot_dinv, cuts, land_pinv)
    knot_dir, land_dir = (knot_z, land_z)
    rho = jnp.sum(knot_resid * knot_z) + jnp.sum(land_resid * land_z)
    for turn in range(ITERS):
        knot_q, land_q = hessian_product(knot_dir, land_dir, jac_knot, jac_land, obs_knot, obs_slot, obs_count, send_list, knot_damp, land_damp)
        alpha = rho / (jnp.sum(knot_dir * knot_q) + jnp.sum(land_dir * land_q))
        knot_step = knot_step + alpha * knot_dir
        land_step = land_step + alpha * land_dir
        knot_resid = knot_resid - alpha * knot_q
        land_resid = land_resid - alpha * land_q
        if turn + 1 < ITERS:
            knot_z, land_z = precondition(knot_resid, land_resid, couple, knot_dinv, cuts, land_pinv)
            rho_next = jnp.sum(knot_resid * knot_z) + jnp.sum(land_resid * land_z)
            knot_dir = knot_z + rho_next / rho * knot_dir
            land_dir = land_z + rho_next / rho * land_dir
            rho = rho_next
    return (knot_step, land_step, knot_resid, land_resid)
```

```python
import functools
import jax
import jax.numpy as jnp
from jax import lax
from jax.experimental import pallas as pl
from jax.experimental.pallas import tpu as pltpu
from jax.sharding import PartitionSpec as P

VB = 4
LB = 64
ITERS = 3
LANES = 128
AXES = ("tm", "lm")
F32 = jnp.float32
BF16 = jnp.bfloat16

NT = (((1,), (1,)), ((), ()))
TN = (((0,), (0,)), ((), ()))
NN = (((1,), (0,)), ((), ()))


def up8(value):
    return (value + 7) // 8 * 8


def bf_dot(left, right, dims):
    return lax.dot_general(left, right, dims, preferred_element_type=F32)


def matvec(tiles, vector):
    total = tiles[0] * vector[0:1]
    for index in range(1, len(tiles)):
        total = total + tiles[index] * vector[index : index + 1]
    return total


def whole_sum(value):
    return jnp.sum(jnp.sum(value, axis=0, keepdims=True), axis=1, keepdims=True)


class Plan:
    def __init__(self, comps, knots, land, rows, n_tm, n_lm, cap, width):
        self.comps, self.knots, self.land, self.rows = comps, knots, land, rows
        self.n_tm, self.n_lm, self.cap = n_tm, n_lm, cap
        self.devices = n_tm * n_lm
        self.slots = self.devices * cap
        self.width = width
        self.field = comps * knots
        self.pairs = land // LANES
        self.blocks = land // LB
        self.zrows = up8(2 * cap)
        self.items = 3
        self.items0 = 3 + 2 * comps
        self.held = -(-self.items // n_lm)
        self.held0 = -(-self.items0 // n_lm)
        self.rw = self.zrows + up8(comps * self.held)
        self.rw0 = self.zrows + up8(comps * self.held0)

    def item_row(self, source, item, rw):
        holder = source * self.n_lm + item % self.n_lm
        return holder * rw + self.zrows + self.comps * (item // self.n_lm)


def col_tiles(ref, plan, k):
    step = plan.comps * plan.knots
    return [
        ref[pl.ds(b * plan.knots + k, plan.comps, stride=step), :] for b in range(plan.comps)
    ]


def row_tiles(ref, plan, k):
    step = plan.comps * plan.knots
    return [
        ref[pl.ds(a * step + k, plan.comps, stride=plan.knots), :] for a in range(plan.comps)
    ]


def local_sweeps(plan, resid_ref, couple_ref, dinv_ref, cuts_ref, zloc_ref, maps=None):
    comps, knots = plan.comps, plan.knots
    lanes = couple_ref.shape[1]
    minus = cuts_ref[...].astype(F32) - 1.0
    carry = None
    basis = []
    if maps is not None:
        rows = lax.broadcasted_iota(jnp.int32, (comps, lanes), 0)
        basis = [(rows == b).astype(F32) for b in range(comps)]
    eye = basis
    scaled, turned, scaled_maps = [], [], []
    energy = jnp.zeros((comps, lanes), F32)
    for k in range(knots):
        value = resid_ref[pl.ds(k, comps, stride=knots), :]
        if carry is not None:
            value = value + carry
        dcol = col_tiles(dinv_ref, plan, k)
        y = matvec(dcol, value)
        scaled.append(y)
        turned.append(matvec(row_tiles(dinv_ref, plan, k), value))
        energy = energy + value * y
        lcol = col_tiles(couple_ref, plan, k)
        gate = minus[k : k + 1]
        carry = gate * matvec(lcol, value)
        if maps is not None:
            scaled_maps.append([matvec(dcol, col) for col in basis])
            basis = [gate * matvec(lcol, col) for col in basis]
    out = carry
    total = basis
    z, u = None, None
    onward, back = [None] * comps, eye
    for k in reversed(range(knots)):
        lrow = row_tiles(couple_ref, plan, k)
        gate = minus[k : k + 1]
        z = scaled[k] if z is None else scaled[k] + gate * matvec(lrow, z)
        u = turned[k] if u is None else turned[k] + gate * matvec(lrow, u)
        zloc_ref[pl.ds(k, comps, stride=knots), :] = z
        if maps is not None:
            onward_ref, back_ref = maps
            onward = [
                scaled_maps[k][b]
                if onward[b] is None
                else scaled_maps[k][b] + gate * matvec(lrow, onward[b])
                for b in range(comps)
            ]
            back = [gate * matvec(lrow, back[b]) for b in range(comps)]
            for b in range(comps):
                spot = pl.ds(b * knots + k, comps, stride=comps * knots)
                onward_ref[spot, :] = onward[b]
                back_ref[spot, :] = back[b]
    return out, z, z + u, energy, total, onward


def scale_land(plan, pinv_ref, land):
    pairs = plan.pairs
    result = []
    for a in range(3):
        total = pinv_ref[pl.ds(3 * a * pairs, pairs), :] * land[0]
        for b in range(1, 3):
            total = total + pinv_ref[pl.ds((3 * a + b) * pairs, pairs), :] * land[b]
        result.append(total)
    return result


def lower_half(shape):
    return lax.broadcasted_iota(jnp.int32, shape, 1) < LB


def roll_half(value):
    return pltpu.roll(value, LB, 1)


def split3(value):
    high = value.astype(BF16)
    rest = value - high.astype(F32)
    mid = rest.astype(BF16)
    low = (rest - mid.astype(F32)).astype(BF16)
    return high, mid, low


def pack_first(plan, rw, held, pick_ref, land_z, scalar, items, place_ref, item_ref, tile_ref, send_ref):
    devices, cap, comps = plan.devices, plan.cap, plan.comps
    half = lower_half(land_z[0].shape)
    z0, z1, z2 = land_z
    r0, r1, r2 = roll_half(z0), roll_half(z1), roll_half(z2)
    zero = jnp.zeros_like(z0)
    first = jnp.concatenate([jnp.where(half, z0, r1), jnp.where(half, r0, z1)], axis=0)
    second = jnp.concatenate([jnp.where(half, z2, zero), jnp.where(half, r2, zero)], axis=0)
    both = jnp.concatenate([first, second], axis=1)
    stacked = jnp.concatenate(list(split3(both)), axis=0)
    pick = pick_ref[...]
    picks = jnp.concatenate([pick, pick, pick], axis=0)
    rows = bf_dot(picks, stacked, TN)
    spot = lax.broadcasted_iota(jnp.int32, (devices, LANES), 1) == LB
    for c in range(cap):
        part = rows[c * devices : (c + 1) * devices]
        tail = part[:, LANES:]
        if c == 0:
            tail = jnp.where(spot, scalar, tail)
        send_ref[pl.ds(c, devices, stride=rw), :] = part[:, :LANES]
        send_ref[pl.ds(cap + c, devices, stride=rw), :] = tail
    for unused in range(2 * cap, plan.zrows):
        send_ref[pl.ds(unused, devices, stride=rw), :] = jnp.zeros((devices, LANES), F32)
    item_ref[...] = jnp.zeros_like(item_ref)
    for index, item in enumerate(items):
        item_ref[index, pl.ds(0, comps), :] = item
    tile_ref[...] = jnp.zeros_like(tile_ref)
    mine = place_ref[1]
    for k in range(held):
        tile_ref[pl.ds(comps * k, comps), :] = item_ref[k * plan.n_lm + mine, pl.ds(0, comps), :]
    tile = tile_ref[...]
    for d in range(devices):
        send_ref[pl.ds(d * rw + plan.zrows, rw - plan.zrows), :] = tile


def leader(place_ref):
    return (place_ref[1] == 0).astype(F32)


def start_kernel(
    plan,
    place_ref,
    resid_ref,
    rhs_ref,
    couple_ref,
    dinv_ref,
    cuts_ref,
    pinv_ref,
    damp_ref,
    list_ref,
    send_ref,
    zloc_ref,
    onward_ref,
    back_ref,
    land_ref,
    land_z_ref,
    land_damp_ref,
    land_pinv_ref,
    pick_ref,
    item_ref,
    tile_ref,
):
    pairs = plan.pairs
    for j in range(pairs):
        cut = pl.ds(j * LANES, LANES)
        land_ref[pl.ds(j, 3, stride=pairs), :] = rhs_ref[:, cut]
        land_damp_ref[pl.ds(j, 3, stride=pairs), :] = damp_ref[:, cut]
        for a in range(3):
            land_pinv_ref[pl.ds(3 * a * pairs + j, 3, stride=pairs), :] = pinv_ref[a, :, cut]
    index = lax.broadcasted_iota(jnp.int32, (plan.blocks, plan.slots), 0)
    wanted = list_ref[...]
    wanted = (wanted % 2) * pairs + wanted // 2
    pick_ref[...] = (index == wanted).astype(F32).astype(BF16)
    land = [land_ref[pl.ds(a * pairs, pairs), :] for a in range(3)]
    land_z = scale_land(plan, land_pinv_ref, land)
    energy = jnp.zeros((pairs, LANES), F32)
    for a in range(3):
        land_z_ref[pl.ds(a * pairs, pairs), :] = land_z[a]
        energy = energy + land[a] * land_z[a]
    out, v1, v12, knot_energy, total, inner = local_sweeps(
        plan, resid_ref, couple_ref, dinv_ref, cuts_ref, zloc_ref, (onward_ref, back_ref)
    )
    scalar = whole_sum(energy) + leader(place_ref) * whole_sum(knot_energy)
    pack_first(
        plan, plan.rw0, plan.held0, pick_ref, land_z, scalar, [out, v1, v12] + total + inner,
        place_ref, item_ref, tile_ref, send_ref,
    )


def product_kernel(first, plan, *refs):
    refs = list(refs)
    place_ref, recv_ref, zloc_ref, onward_ref, back_ref, land_z_ref = refs[:6]
    knot_damp_ref, land_damp_ref, jk_ref, jl_ref, link_ref, sel_ref, spread_ref = refs[6:13]
    refs = refs[13:]
    if first:
        rw = plan.rw0
        outs = refs
    else:
        rw = plan.rw
        chain_in_ref, rho_in_ref, knot_in_ref, land_in_ref, slot_in_ref = refs[:5]
        outs = refs[5:]
    send_ref, part_ref, rho_ref, knot_ref, land_ref, slot_ref = outs[:6]
    outs = outs[6:]
    if first:
        chain_ref = outs[0]
        outs = outs[1:]
    else:
        chain_ref = chain_in_ref
    entry_ref, arrive_ref, wide_ref = outs
    comps, knots, cap, devices = plan.comps, plan.knots, plan.cap, plan.devices
    lanes = zloc_ref.shape[1]
    square = comps * comps

    if first:
        for s in range(plan.n_tm):
            for m in range(2 * comps):
                spot = plan.item_row(s, 3 + m, rw)
                chain_ref[pl.ds(s * 2 * square + m * comps, comps), :] = recv_ref[
                    pl.ds(spot, comps), :
                ]

    def item(s, index):
        return recv_ref[pl.ds(plan.item_row(s, index, rw), comps), :]

    incoming = None
    firsts = []
    heat = jnp.zeros((comps, lanes), F32)
    for s in range(plan.n_tm):
        base = s * 2 * square
        v1 = item(s, 1)
        if incoming is None:
            entry_ref[s, pl.ds(0, comps), :] = jnp.zeros((comps, lanes), F32)
            firsts.append(v1)
            incoming = item(s, 0)
        else:
            entry_ref[s, pl.ds(0, comps), :] = incoming
            inner = [chain_ref[pl.ds(base + square + b * comps, comps), :] for b in range(comps)]
            pushed = matvec(inner, incoming)
            heat = heat + incoming * (item(s, 2) + pushed)
            firsts.append(v1 + pushed)
            if s + 1 < plan.n_tm:
                total = [chain_ref[pl.ds(base + b * comps, comps), :] for b in range(comps)]
                incoming = matvec(total, incoming) + item(s, 0)
    arriving = None
    for s in reversed(range(plan.n_tm)):
        base = s * 2 * square
        if arriving is None:
            arrive_ref[s, pl.ds(0, comps), :] = jnp.zeros((comps, lanes), F32)
            arriving = firsts[s]
        else:
            arrive_ref[s, pl.ds(0, comps), :] = arriving
            if s > 0:
                back = [
                    chain_ref[pl.ds(base + a, comps, stride=comps), :] for a in range(comps)
                ]
                arriving = firsts[s] + matvec(back, arriving)

    lane = lax.broadcasted_iota(jnp.int32, (devices, LANES), 1)
    tails = [recv_ref[pl.ds(cap + c, devices, stride=rw), :] for c in range(cap)]
    heads = [recv_ref[pl.ds(c, devices, stride=rw), :] for c in range(cap)]
    rho = whole_sum(jnp.where(lane == LB, tails[0], 0.0)) + whole_sum(heat)
    rho_ref[...] = jnp.broadcast_to(rho, rho_ref.shape)
    if not first:
        beta = rho / rho_in_ref[0:1, 0:1]
    half = lane < LB
    tails = [jnp.where(half, tail, 0.0) for tail in tails]
    slot_dir = []
    for index, rows in enumerate(heads + tails):
        spot = pl.ds(index * devices, devices)
        if not first:
            rows = rows + beta * slot_in_ref[spot, :]
        slot_ref[spot, :] = rows
        slot_dir.append(rows)
    land_dir = land_z_ref[...]
    if not first:
        land_dir = land_dir + beta * land_in_ref[...]
    land_ref[...] = land_dir
    heat = whole_sum(land_damp_ref[...] * land_dir * land_dir)

    mine = place_ref[0]
    entry = entry_ref[mine, pl.ds(0, comps), :]
    arrive = arrive_ref[mine, pl.ds(0, comps), :]
    for a in range(comps):
        total = zloc_ref[pl.ds(a * knots, knots), :]
        for b in range(comps):
            spot = pl.ds((a * comps + b) * knots, knots)
            total = total + onward_ref[spot, :] * entry[b : b + 1]
            total = total + back_ref[spot, :] * arrive[b : b + 1]
        if not first:
            total = total + beta * knot_in_ref[pl.ds(a * knots, knots), :]
        knot_ref[pl.ds(a * knots, knots), :] = total
    knot_dir = knot_ref[...]
    heat = heat + leader(place_ref) * whole_sum(knot_damp_ref[...] * knot_dir * knot_dir)

    groups = lanes // VB
    narrow = knot_dir.astype(BF16)
    padded = jnp.concatenate([narrow, jnp.zeros((LANES - plan.field, lanes), BF16)], axis=0)
    turned = bf_dot(sel_ref[...], padded, NT).astype(BF16)
    joined = jnp.concatenate(
        [turned[i * groups : (i + 1) * groups] for i in range(VB)], axis=1
    )
    knot_rows = bf_dot(joined, spread_ref[...], NN).astype(BF16)
    slot_rows = jnp.concatenate(
        [
            jnp.concatenate(slot_dir[:cap], axis=0).astype(BF16),
            jnp.concatenate(slot_dir[cap:], axis=0).astype(BF16)[:, :LB],
        ],
        axis=1,
    )
    chunk = 512
    knot_total, land_total = None, None
    for start in range(0, plan.rows, chunk):
        cut = pl.ds(start, chunk)
        jk, jl = jk_ref[cut, :], jl_ref[cut, :]
        near = bf_dot(knot_rows, jk, NT)
        far = bf_dot(slot_rows, jl, NT)
        knot_hit = lax.broadcasted_iota(jnp.int32, near.shape, 0) == link_ref[0:1, cut]
        slot_hit = lax.broadcasted_iota(jnp.int32, far.shape, 0) == link_ref[1:2, cut]
        resid = jnp.sum(jnp.where(knot_hit, near, 0.0), axis=0, keepdims=True) + jnp.sum(
            jnp.where(slot_hit, far, 0.0), axis=0, keepdims=True
        )
        knot_side = jnp.where(knot_hit, resid, 0.0).astype(BF16)
        slot_side = jnp.where(slot_hit, resid, 0.0).astype(BF16)
        knot_term = bf_dot(knot_side, jk, NN)
        land_term = bf_dot(slot_side, jl, NN)
        knot_total = knot_term if knot_total is None else knot_total + knot_term
        land_total = land_term if land_total is None else land_total + land_term

    parted = bf_dot(knot_total.astype(BF16), spread_ref[...], NT).astype(BF16)
    piled = jnp.concatenate(
        [parted[:, i * LANES : (i + 1) * LANES] for i in range(VB)], axis=0
    )
    part = bf_dot(piled, sel_ref[...], TN)[: plan.field]
    part_ref[...] = part.astype(BF16)
    heat = heat + whole_sum(part * knot_dir)
    land_total = land_total.astype(BF16).astype(F32)
    lead_rows = land_total[:, :LANES]
    tail_rows = jnp.concatenate(
        [land_total[:, LANES:], jnp.zeros((plan.slots, LANES - LB), F32)], axis=1
    )
    sums = jnp.zeros((devices, LANES), F32)
    for c in range(cap):
        cut = slice(c * devices, (c + 1) * devices)
        sums = sums + lead_rows[cut] * slot_dir[c] + tail_rows[cut] * slot_dir[cap + c]
    heat = heat + whole_sum(sums)
    high, mid, low = [piece.astype(F32) for piece in split3(heat)]
    if 2 * cap < plan.zrows:
        wide_ref[...] = jnp.zeros_like(wide_ref)
    for c in range(cap):
        cut = slice(c * devices, (c + 1) * devices)
        tail = tail_rows[cut]
        if c == 0:
            tail = jnp.where(lane == LB, high, tail)
            tail = jnp.where(lane == LB + 1, mid, tail)
            tail = jnp.where(lane == LB + 2, low, tail)
        wide_ref[pl.ds(c, devices, stride=plan.zrows), :] = lead_rows[cut]
        wide_ref[pl.ds(cap + c, devices, stride=plan.zrows), :] = tail
    send_ref[...] = wide_ref[...].astype(BF16)


def update_kernel(first, last, plan, *refs):
    refs = list(refs)
    place_ref, recv_ref = refs[:2]
    part_refs = refs[2 : 2 + plan.n_lm]
    refs = refs[2 + plan.n_lm :]
    rho_ref, knot_dir_ref, land_dir_ref, knot_resid_ref, land_resid_ref = refs[:5]
    knot_damp_ref, land_damp_ref, pick_ref = refs[5:8]
    refs = refs[8:]
    if not first:
        knot_step_ref, land_step_ref = refs[:2]
        refs = refs[2:]
    if not last:
        couple_ref, dinv_ref, cuts_ref, pinv_ref = refs[:4]
        refs = refs[4:]
    knot_step_out, land_step_out, knot_resid_out, land_resid_out = refs[:4]
    refs = refs[4:]
    if not last:
        send_ref, zloc_ref, land_z_ref = refs[:3]
        refs = refs[3:]
        wide_ref, item_ref, tile_ref = refs
    else:
        wide_ref, step_tmp, resid_tmp = refs
    cap, devices, pairs = plan.cap, plan.devices, plan.pairs

    wide_ref[...] = recv_ref[...].astype(F32)
    lane = lax.broadcasted_iota(jnp.int32, (devices, LANES), 1)
    heads = [wide_ref[pl.ds(c, devices, stride=plan.zrows), :] for c in range(cap)]
    tails = [wide_ref[pl.ds(cap + c, devices, stride=plan.zrows), :] for c in range(cap)]
    scalars = (lane >= LB) & (lane < LB + 3)
    alpha = rho_ref[0:1, 0:1] / whole_sum(jnp.where(scalars, tails[0], 0.0))
    lead = bf_dot(pick_ref[...], jnp.concatenate(heads, axis=0).astype(BF16), NN)
    tail = bf_dot(pick_ref[...], jnp.concatenate(tails, axis=0).astype(BF16), NN)
    half = lower_half((pairs, LANES))
    even, odd = lead[:pairs], lead[pairs:]
    grads = [
        jnp.where(half, even, roll_half(odd)),
        jnp.where(half, roll_half(even), odd),
        jnp.where(half, tail[:pairs], roll_half(tail[pairs:])),
    ]

    parts = [ref[...].astype(F32) for ref in part_refs]
    while len(parts) > 1:
        parts = [parts[i] + parts[i + 1] for i in range(0, len(parts), 2)]
    knot_dir = knot_dir_ref[...]
    knot_q = parts[0] + knot_damp_ref[...] * knot_dir
    step = alpha * knot_dir
    knot_step_out[...] = step if first else knot_step_ref[...] + step
    knot_resid_out[...] = knot_resid_ref[...] - alpha * knot_q

    step_to, resid_to = (step_tmp, resid_tmp) if last else (land_step_out, land_resid_out)
    land = []
    for a in range(3):
        spot = pl.ds(a * pairs, pairs)
        along = land_dir_ref[spot, :]
        q = grads[a] + land_damp_ref[spot, :] * along
        step = alpha * along
        step_to[spot, :] = step if first else land_step_ref[spot, :] + step
        value = land_resid_ref[spot, :] - alpha * q
        resid_to[spot, :] = value
        land.append(value)
    if last:
        for j in range(pairs):
            cut = pl.ds(j * LANES, LANES)
            land_step_out[:, cut] = step_tmp[pl.ds(j, 3, stride=pairs), :]
            land_resid_out[:, cut] = resid_tmp[pl.ds(j, 3, stride=pairs), :]
        return
    land_z = scale_land(plan, pinv_ref, land)
    energy = jnp.zeros((pairs, LANES), F32)
    for a in range(3):
        land_z_ref[pl.ds(a * pairs, pairs), :] = land_z[a]
        energy = energy + land[a] * land_z[a]
    out, v1, v12, knot_energy, _, _ = local_sweeps(
        plan, knot_resid_out, couple_ref, dinv_ref, cuts_ref, zloc_ref
    )
    scalar = whole_sum(energy) + leader(place_ref) * whole_sum(knot_energy)
    pack_first(
        plan, plan.rw, plan.held, pick_ref, land_z, scalar, [out, v1, v12],
        place_ref, item_ref, tile_ref, send_ref,
    )


def call(kernel, name, outs, args, scratch):
    vmem = pl.BlockSpec(memory_space=pltpu.VMEM)
    smem = pl.BlockSpec(memory_space=pltpu.SMEM)
    return pl.pallas_call(
        kernel,
        name=name,
        out_shape=[jax.ShapeDtypeStruct(shape, dtype) for shape, dtype in outs],
        in_specs=[smem] + [vmem] * (len(args) - 1),
        out_specs=[vmem] * len(outs),
        scratch_shapes=scratch,
        compiler_params=pltpu.CompilerParams(vmem_limit_bytes=24 << 20),
    )(*args)


def exchange(blocks, devices):
    rows = blocks.shape[0] // devices
    shaped = blocks.reshape(devices, rows, LANES)
    moved = lax.all_to_all(shaped, AXES, split_axis=0, concat_axis=0, tiled=True)
    return moved.reshape(blocks.shape)


def swap(value, mask):
    count = lax.axis_size("lm")
    return lax.ppermute(value, "lm", [(i, i ^ mask) for i in range(count)])


def on_device(
    knot_right_side,
    land_rhs,
    jac_knot,
    jac_land,
    obs_knot,
    obs_slot,
    obs_count,
    send_list,
    couple,
    knot_dinv,
    cuts,
    land_pinv,
    knot_damp,
    land_damp,
):
    comps, knots, vehicles = knot_right_side.shape
    observed, height, knot_width = jac_knot.shape
    rows = observed * height
    cap = send_list.shape[2]
    n_tm, n_lm = lax.axis_size("tm"), lax.axis_size("lm")
    plan = Plan(
        comps, knots, land_rhs.shape[1], rows, n_tm, n_lm, cap, jac_land.shape[2]
    )
    devices, slots, field, pairs = plan.devices, plan.slots, plan.field, plan.pairs
    square = comps * comps

    place = jnp.stack([lax.axis_index("tm"), lax.axis_index("lm")]).astype(jnp.int32)
    resid = knot_right_side.reshape(field, vehicles)
    couple = couple.reshape(square * knots, vehicles)
    dinv = knot_dinv.reshape(square * knots, vehicles)
    knot_damp = knot_damp.reshape(field, vehicles)
    jk = jac_knot.reshape(rows, knot_width)
    jl = jac_land.reshape(rows, jac_land.shape[2])
    listed = jnp.transpose(send_list[0]).reshape(1, slots)

    live = jnp.arange(height, dtype=jnp.int32)[None, :] < obs_count[:, None]
    slot = (obs_slot % cap) * devices + obs_slot // cap
    links = jnp.stack(
        [jnp.where(live, obs_knot[:, None], -1), jnp.where(live, slot[:, None], -1)]
    ).reshape(2, rows)

    groups = vehicles // VB
    lane = jnp.arange(vehicles, dtype=jnp.int32)
    ordered = (lane % groups) * VB + lane // groups
    sel = (ordered[:, None] == lane[None, :]).astype(BF16)
    spot = jnp.arange(VB * LANES, dtype=jnp.int32)
    aim = jnp.where(spot % LANES < field, (spot % LANES) * VB + spot // LANES, -1)
    spread = (aim[:, None] == jnp.arange(knot_width, dtype=jnp.int32)[None, :]).astype(BF16)

    def items_scratch(held):
        return [
            pltpu.VMEM((held * n_lm, 8, LANES), F32),
            pltpu.VMEM((up8(comps * held), LANES), F32),
        ]

    send, zloc, onward, back, land_resid, land_z, damp, pinv, pick = call(
        functools.partial(start_kernel, plan),
        "start",
        [
            ((devices * plan.rw0, LANES), F32),
            ((field, vehicles), F32),
            ((square * knots, vehicles), F32),
            ((square * knots, vehicles), F32),
            ((3 * pairs, LANES), F32),
            ((3 * pairs, LANES), F32),
            ((3 * pairs, LANES), F32),
            ((9 * pairs, LANES), F32),
            ((plan.blocks, slots), BF16),
        ],
        [place, resid, land_rhs, couple, dinv, cuts, land_pinv, land_damp, listed],
        items_scratch(plan.held0),
    )
    state = None
    chain = None
    steps = None
    for turn in range(ITERS):
        first, last = turn == 0, turn == ITERS - 1
        recv = exchange(send, devices)
        args = [place, recv, zloc, onward, back, land_z, knot_damp, damp, jk, jl, links, sel, spread]
        outs = [
            ((devices * plan.zrows, LANES), BF16),
            ((field, vehicles), BF16),
            ((8, LANES), F32),
            ((field, vehicles), F32),
            ((3 * pairs, LANES), F32),
            ((2 * slots, LANES), F32),
        ]
        if first:
            outs.append(((n_tm * 2 * square, vehicles), F32))
        else:
            args += [chain] + list(state)
        results = call(
            functools.partial(product_kernel, first, plan),
            "product_first" if first else "product",
            outs,
            args,
            [
                pltpu.VMEM((n_tm, 8, vehicles), F32),
                pltpu.VMEM((n_tm, 8, vehicles), F32),
                pltpu.VMEM((devices * plan.zrows, LANES), F32),
            ],
        )
        send, part = results[:2]
        state = results[2:6]
        if first:
            chain = results[6]
        rho, knot_dir, land_dir, _ = state
        parts = [part] + [swap(part, mask) for mask in range(1, n_lm)]
        recv = exchange(send, devices)
        args = [place, recv] + parts
        args += [rho, knot_dir, land_dir, resid, land_resid, knot_damp, damp, pick]
        if not first:
            args += list(steps)
        wide = pltpu.VMEM((devices * plan.zrows, LANES), F32)
        if last:
            outs = [((field, vehicles), F32), ((3, plan.land), F32)] * 2
            scratch = [wide] + [pltpu.VMEM((3 * pairs, LANES), F32)] * 2
        else:
            args += [couple, dinv, cuts, pinv]
            outs = [((field, vehicles), F32), ((3 * pairs, LANES), F32)] * 2
            outs += [
                ((devices * plan.rw, LANES), F32),
                ((field, vehicles), F32),
                ((3 * pairs, LANES), F32),
            ]
            scratch = [wide] + items_scratch(plan.held)
        results = call(
            functools.partial(update_kernel, first, last, plan),
            "update_last" if last else "update",
            outs,
            args,
            scratch,
        )
        steps = results[:2]
        resid, land_resid = results[2:4]
        if not last:
            send, zloc, land_z = results[4:]
    shape = (comps, knots, vehicles)
    return (steps[0].reshape(shape), steps[1], resid.reshape(shape), land_resid)


def solution(mesh):
    return jax.shard_map(
        on_device,
        mesh=mesh,
        in_specs=(
            P(None, "tm", None),
            P(None, ("tm", "lm")),
            P(("tm", "lm"), None, None),
            P(("tm", "lm"), None, None),
            P(("tm", "lm")),
            P(("tm", "lm")),
            P(("tm", "lm")),
            P(("tm", "lm"), None, None),
            P(None, None, "tm", None),
            P(None, None, "tm", None),
            P("tm", None),
            P(None, None, ("tm", "lm")),
            P(None, "tm", None),
            P(None, ("tm", "lm")),
        ),
        out_specs=(
            P(None, "tm", None),
            P(None, ("tm", "lm")),
            P(None, "tm", None),
            P(None, ("tm", "lm")),
        ),
        check_vma=False,
    )
```

```python
import functools
import jax
import jax.numpy as jnp
from jax import lax
from jax.experimental import pallas as pl
from jax.experimental.pallas import tpu as pltpu
from jax.sharding import PartitionSpec as P

VB = 4
LB = 64
ITERS = 3
LANES = 128
AXES = ("tm", "lm")
F32 = jnp.float32
BF16 = jnp.bfloat16

NT = (((1,), (1,)), ((), ()))
TN = (((0,), (0,)), ((), ()))
NN = (((1,), (0,)), ((), ()))


def up8(value):
    return (value + 7) // 8 * 8


def bf_dot(left, right, dims):
    return lax.dot_general(left, right, dims, preferred_element_type=F32)


def matvec(tiles, vector):
    total = tiles[0] * vector[0:1]
    for index in range(1, len(tiles)):
        total = total + tiles[index] * vector[index : index + 1]
    return total


def whole_sum(value):
    return jnp.sum(jnp.sum(value, axis=0, keepdims=True), axis=1, keepdims=True)


class Plan:
    def __init__(self, comps, knots, land, rows, n_tm, n_lm, cap, width):
        self.comps, self.knots, self.land, self.rows = comps, knots, land, rows
        self.n_tm, self.n_lm, self.cap = n_tm, n_lm, cap
        self.devices = n_tm * n_lm
        self.slots = self.devices * cap
        self.width = width
        self.field = comps * knots
        self.pairs = land // LANES
        self.blocks = land // LB
        self.zrows = up8(2 * cap)
        self.items = 3
        self.items0 = 3 + 2 * comps
        self.held = -(-self.items // n_lm)
        self.held0 = -(-self.items0 // n_lm)
        self.rw = self.zrows + up8(comps * self.held)
        self.rw0 = self.zrows + up8(comps * self.held0)

    def item_row(self, source, item, rw):
        holder = source * self.n_lm + item % self.n_lm
        return holder * rw + self.zrows + self.comps * (item // self.n_lm)


def col_tiles(ref, plan, k):
    step = plan.comps * plan.knots
    return [
        ref[pl.ds(b * plan.knots + k, plan.comps, stride=step), :] for b in range(plan.comps)
    ]


def row_tiles(ref, plan, k):
    step = plan.comps * plan.knots
    return [
        ref[pl.ds(a * step + k, plan.comps, stride=plan.knots), :] for a in range(plan.comps)
    ]


def local_sweeps(plan, resid_ref, couple_ref, dinv_ref, cuts_ref, zloc_ref, maps=None):
    comps, knots = plan.comps, plan.knots
    lanes = couple_ref.shape[1]
    minus = cuts_ref[...].astype(F32) - 1.0
    carry = None
    basis = []
    if maps is not None:
        rows = lax.broadcasted_iota(jnp.int32, (comps, lanes), 0)
        basis = [(rows == b).astype(F32) for b in range(comps)]
    eye = basis
    scaled, turned, scaled_maps = [], [], []
    energy = jnp.zeros((comps, lanes), F32)
    for k in range(knots):
        value = resid_ref[pl.ds(k, comps, stride=knots), :]
        if carry is not None:
            value = value + carry
        dcol = col_tiles(dinv_ref, plan, k)
        y = matvec(dcol, value)
        scaled.append(y)
        turned.append(matvec(row_tiles(dinv_ref, plan, k), value))
        energy = energy + value * y
        lcol = col_tiles(couple_ref, plan, k)
        gate = minus[k : k + 1]
        carry = gate * matvec(lcol, value)
        if maps is not None:
            scaled_maps.append([matvec(dcol, col) for col in basis])
            basis = [gate * matvec(lcol, col) for col in basis]
    out = carry
    total = basis
    z, u = None, None
    onward, back = [None] * comps, eye
    for k in reversed(range(knots)):
        lrow = row_tiles(couple_ref, plan, k)
        gate = minus[k : k + 1]
        z = scaled[k] if z is None else scaled[k] + gate * matvec(lrow, z)
        u = turned[k] if u is None else turned[k] + gate * matvec(lrow, u)
        zloc_ref[pl.ds(k, comps, stride=knots), :] = z
        if maps is not None:
            onward_ref, back_ref = maps
            onward = [
                scaled_maps[k][b]
                if onward[b] is None
                else scaled_maps[k][b] + gate * matvec(lrow, onward[b])
                for b in range(comps)
            ]
            back = [gate * matvec(lrow, back[b]) for b in range(comps)]
            for b in range(comps):
                spot = pl.ds(b * knots + k, comps, stride=comps * knots)
                onward_ref[spot, :] = onward[b]
                back_ref[spot, :] = back[b]
    return out, z, z + u, energy, total, onward


def scale_land(plan, pinv_ref, land):
    pairs = plan.pairs
    result = []
    for a in range(3):
        total = pinv_ref[pl.ds(3 * a * pairs, pairs), :] * land[0]
        for b in range(1, 3):
            total = total + pinv_ref[pl.ds((3 * a + b) * pairs, pairs), :] * land[b]
        result.append(total)
    return result


def lower_half(shape):
    return lax.broadcasted_iota(jnp.int32, shape, 1) < LB


def roll_half(value):
    return pltpu.roll(value, LB, 1)


def split3(value):
    high = value.astype(BF16)
    rest = value - high.astype(F32)
    mid = rest.astype(BF16)
    low = (rest - mid.astype(F32)).astype(BF16)
    return high, mid, low


def pack_first(plan, rw, held, pick_ref, land_z, scalar, items, place_ref, item_ref, tile_ref, send_ref):
    devices, cap, comps = plan.devices, plan.cap, plan.comps
    half = lower_half(land_z[0].shape)
    z0, z1, z2 = land_z
    r0, r1, r2 = roll_half(z0), roll_half(z1), roll_half(z2)
    zero = jnp.zeros_like(z0)
    first = jnp.concatenate([jnp.where(half, z0, r1), jnp.where(half, r0, z1)], axis=0)
    second = jnp.concatenate([jnp.where(half, z2, zero), jnp.where(half, r2, zero)], axis=0)
    both = jnp.concatenate([first, second], axis=1)
    stacked = jnp.concatenate(list(split3(both)), axis=0)
    pick = pick_ref[...]
    picks = jnp.concatenate([pick, pick, pick], axis=0)
    rows = bf_dot(picks, stacked, TN)
    spot = lax.broadcasted_iota(jnp.int32, (devices, LANES), 1) == LB
    for c in range(cap):
        part = rows[c * devices : (c + 1) * devices]
        tail = part[:, LANES:]
        if c == 0:
            tail = jnp.where(spot, scalar, tail)
        send_ref[pl.ds(c, devices, stride=rw), :] = part[:, :LANES]
        send_ref[pl.ds(cap + c, devices, stride=rw), :] = tail
    for unused in range(2 * cap, plan.zrows):
        send_ref[pl.ds(unused, devices, stride=rw), :] = jnp.zeros((devices, LANES), F32)
    item_ref[...] = jnp.zeros_like(item_ref)
    for index, item in enumerate(items):
        item_ref[index, pl.ds(0, comps), :] = item
    tile_ref[...] = jnp.zeros_like(tile_ref)
    mine = place_ref[1]
    for k in range(held):
        tile_ref[pl.ds(comps * k, comps), :] = item_ref[k * plan.n_lm + mine, pl.ds(0, comps), :]
    tile = tile_ref[...]
    for d in range(devices):
        send_ref[pl.ds(d * rw + plan.zrows, rw - plan.zrows), :] = tile


def leader(place_ref):
    return (place_ref[1] == 0).astype(F32)


def start_kernel(
    plan,
    place_ref,
    resid_ref,
    rhs_ref,
    couple_ref,
    dinv_ref,
    cuts_ref,
    pinv_ref,
    damp_ref,
    list_ref,
    send_ref,
    zloc_ref,
    onward_ref,
    back_ref,
    land_ref,
    land_z_ref,
    land_damp_ref,
    land_pinv_ref,
    pick_ref,
    item_ref,
    tile_ref,
):
    pairs = plan.pairs
    for j in range(pairs):
        cut = pl.ds(j * LANES, LANES)
        land_ref[pl.ds(j, 3, stride=pairs), :] = rhs_ref[:, cut]
        land_damp_ref[pl.ds(j, 3, stride=pairs), :] = damp_ref[:, cut]
        for a in range(3):
            land_pinv_ref[pl.ds(3 * a * pairs + j, 3, stride=pairs), :] = pinv_ref[a, :, cut]
    index = lax.broadcasted_iota(jnp.int32, (plan.blocks, plan.slots), 0)
    wanted = list_ref[...]
    wanted = (wanted % 2) * pairs + wanted // 2
    pick_ref[...] = (index == wanted).astype(F32).astype(BF16)
    land = [land_ref[pl.ds(a * pairs, pairs), :] for a in range(3)]
    land_z = scale_land(plan, land_pinv_ref, land)
    energy = jnp.zeros((pairs, LANES), F32)
    for a in range(3):
        land_z_ref[pl.ds(a * pairs, pairs), :] = land_z[a]
        energy = energy + land[a] * land_z[a]
    out, v1, v12, knot_energy, total, inner = local_sweeps(
        plan, resid_ref, couple_ref, dinv_ref, cuts_ref, zloc_ref, (onward_ref, back_ref)
    )
    scalar = whole_sum(energy) + leader(place_ref) * whole_sum(knot_energy)
    pack_first(
        plan, plan.rw0, plan.held0, pick_ref, land_z, scalar, [out, v1, v12] + total + inner,
        place_ref, item_ref, tile_ref, send_ref,
    )


def product_kernel(first, plan, *refs):
    refs = list(refs)
    place_ref, recv_ref, zloc_ref, onward_ref, back_ref, land_z_ref = refs[:6]
    knot_damp_ref, land_damp_ref, jk_ref, jl_ref, link_ref, sel_ref, spread_ref = refs[6:13]
    refs = refs[13:]
    if first:
        rw = plan.rw0
        outs = refs
    else:
        rw = plan.rw
        chain_in_ref, rho_in_ref, knot_in_ref, land_in_ref, slot_in_ref = refs[:5]
        outs = refs[5:]
    send_ref, part_ref, rho_ref, knot_ref, land_ref, slot_ref = outs[:6]
    outs = outs[6:]
    if first:
        chain_ref = outs[0]
        outs = outs[1:]
    else:
        chain_ref = chain_in_ref
    entry_ref, arrive_ref, wide_ref = outs
    comps, knots, cap, devices = plan.comps, plan.knots, plan.cap, plan.devices
    lanes = zloc_ref.shape[1]
    square = comps * comps

    if first:
        for s in range(plan.n_tm):
            for m in range(2 * comps):
                spot = plan.item_row(s, 3 + m, rw)
                chain_ref[pl.ds(s * 2 * square + m * comps, comps), :] = recv_ref[
                    pl.ds(spot, comps), :
                ]

    def item(s, index):
        return recv_ref[pl.ds(plan.item_row(s, index, rw), comps), :]

    incoming = None
    firsts = []
    heat = jnp.zeros((comps, lanes), F32)
    for s in range(plan.n_tm):
        base = s * 2 * square
        v1 = item(s, 1)
        if incoming is None:
            entry_ref[s, pl.ds(0, comps), :] = jnp.zeros((comps, lanes), F32)
            firsts.append(v1)
            incoming = item(s, 0)
        else:
            entry_ref[s, pl.ds(0, comps), :] = incoming
            inner = [chain_ref[pl.ds(base + square + b * comps, comps), :] for b in range(comps)]
            pushed = matvec(inner, incoming)
            heat = heat + incoming * (item(s, 2) + pushed)
            firsts.append(v1 + pushed)
            if s + 1 < plan.n_tm:
                total = [chain_ref[pl.ds(base + b * comps, comps), :] for b in range(comps)]
                incoming = matvec(total, incoming) + item(s, 0)
    arriving = None
    for s in reversed(range(plan.n_tm)):
        base = s * 2 * square
        if arriving is None:
            arrive_ref[s, pl.ds(0, comps), :] = jnp.zeros((comps, lanes), F32)
            arriving = firsts[s]
        else:
            arrive_ref[s, pl.ds(0, comps), :] = arriving
            if s > 0:
                back = [
                    chain_ref[pl.ds(base + a, comps, stride=comps), :] for a in range(comps)
                ]
                arriving = firsts[s] + matvec(back, arriving)

    lane = lax.broadcasted_iota(jnp.int32, (devices, LANES), 1)
    tails = [recv_ref[pl.ds(cap + c, devices, stride=rw), :] for c in range(cap)]
    heads = [recv_ref[pl.ds(c, devices, stride=rw), :] for c in range(cap)]
    rho = whole_sum(jnp.where(lane == LB, tails[0], 0.0)) + whole_sum(heat)
    rho_ref[...] = jnp.broadcast_to(rho, rho_ref.shape)
    if not first:
        beta = rho / rho_in_ref[0:1, 0:1]
    half = lane < LB
    tails = [jnp.where(half, tail, 0.0) for tail in tails]
    slot_dir = []
    for index, rows in enumerate(heads + tails):
        spot = pl.ds(index * devices, devices)
        if not first:
            rows = rows + beta * slot_in_ref[spot, :]
        slot_ref[spot, :] = rows
        slot_dir.append(rows)
    land_dir = land_z_ref[...]
    if not first:
        land_dir = land_dir + beta * land_in_ref[...]
    land_ref[...] = land_dir
    heat = whole_sum(land_damp_ref[...] * land_dir * land_dir)

    mine = place_ref[0]
    entry = entry_ref[mine, pl.ds(0, comps), :]
    arrive = arrive_ref[mine, pl.ds(0, comps), :]
    for a in range(comps):
        total = zloc_ref[pl.ds(a * knots, knots), :]
        for b in range(comps):
            spot = pl.ds((a * comps + b) * knots, knots)
            total = total + onward_ref[spot, :] * entry[b : b + 1]
            total = total + back_ref[spot, :] * arrive[b : b + 1]
        if not first:
            total = total + beta * knot_in_ref[pl.ds(a * knots, knots), :]
        knot_ref[pl.ds(a * knots, knots), :] = total
    knot_dir = knot_ref[...]
    heat = heat + leader(place_ref) * whole_sum(knot_damp_ref[...] * knot_dir * knot_dir)

    groups = lanes // VB
    narrow = knot_dir.astype(BF16)
    padded = jnp.concatenate([narrow, jnp.zeros((LANES - plan.field, lanes), BF16)], axis=0)
    turned = bf_dot(sel_ref[...], padded, NT).astype(BF16)
    joined = jnp.concatenate(
        [turned[i * groups : (i + 1) * groups] for i in range(VB)], axis=1
    )
    knot_rows = bf_dot(joined, spread_ref[...], NN).astype(BF16)
    slot_rows = jnp.concatenate(
        [
            jnp.concatenate(slot_dir[:cap], axis=0).astype(BF16),
            jnp.concatenate(slot_dir[cap:], axis=0).astype(BF16)[:, :LB],
        ],
        axis=1,
    )
    chunk = 512
    knot_total, land_total = None, None
    for start in range(0, plan.rows, chunk):
        cut = pl.ds(start, chunk)
        jk, jl = jk_ref[cut, :], jl_ref[cut, :]
        near = bf_dot(knot_rows, jk, NT)
        far = bf_dot(slot_rows, jl, NT)
        knot_hit = lax.broadcasted_iota(jnp.int32, near.shape, 0) == link_ref[0:1, cut]
        slot_hit = lax.broadcasted_iota(jnp.int32, far.shape, 0) == link_ref[1:2, cut]
        resid = jnp.sum(jnp.where(knot_hit, near, 0.0), axis=0, keepdims=True) + jnp.sum(
            jnp.where(slot_hit, far, 0.0), axis=0, keepdims=True
        )
        knot_side = jnp.where(knot_hit, resid, 0.0).astype(BF16)
        slot_side = jnp.where(slot_hit, resid, 0.0).astype(BF16)
        knot_term = bf_dot(knot_side, jk, NN)
        land_term = bf_dot(slot_side, jl, NN)
        knot_total = knot_term if knot_total is None else knot_total + knot_term
        land_total = land_term if land_total is None else land_total + land_term

    parted = bf_dot(knot_total.astype(BF16), spread_ref[...], NT).astype(BF16)
    piled = jnp.concatenate(
        [parted[:, i * LANES : (i + 1) * LANES] for i in range(VB)], axis=0
    )
    part = bf_dot(piled, sel_ref[...], TN)[: plan.field]
    part_ref[...] = part.astype(BF16)
    heat = heat + whole_sum(part * knot_dir)
    land_total = land_total.astype(BF16).astype(F32)
    lead_rows = land_total[:, :LANES]
    tail_rows = jnp.concatenate(
        [land_total[:, LANES:], jnp.zeros((plan.slots, LANES - LB), F32)], axis=1
    )
    sums = jnp.zeros((devices, LANES), F32)
    for c in range(cap):
        cut = slice(c * devices, (c + 1) * devices)
        sums = sums + lead_rows[cut] * slot_dir[c] + tail_rows[cut] * slot_dir[cap + c]
    heat = heat + whole_sum(sums)
    high, mid, low = [piece.astype(F32) for piece in split3(heat)]
    if 2 * cap < plan.zrows:
        wide_ref[...] = jnp.zeros_like(wide_ref)
    for c in range(cap):
        cut = slice(c * devices, (c + 1) * devices)
        tail = tail_rows[cut]
        if c == 0:
            tail = jnp.where(lane == LB, high, tail)
            tail = jnp.where(lane == LB + 1, mid, tail)
            tail = jnp.where(lane == LB + 2, low, tail)
        wide_ref[pl.ds(c, devices, stride=plan.zrows), :] = lead_rows[cut]
        wide_ref[pl.ds(cap + c, devices, stride=plan.zrows), :] = tail
    send_ref[...] = wide_ref[...].astype(BF16)


def update_kernel(first, last, plan, *refs):
    refs = list(refs)
    place_ref, recv_ref = refs[:2]
    part_refs = refs[2 : 2 + plan.n_lm]
    refs = refs[2 + plan.n_lm :]
    rho_ref, knot_dir_ref, land_dir_ref, knot_resid_ref, land_resid_ref = refs[:5]
    knot_damp_ref, land_damp_ref, pick_ref = refs[5:8]
    refs = refs[8:]
    if not first:
        knot_step_ref, land_step_ref = refs[:2]
        refs = refs[2:]
    if not last:
        couple_ref, dinv_ref, cuts_ref, pinv_ref = refs[:4]
        refs = refs[4:]
    knot_step_out, land_step_out, knot_resid_out, land_resid_out = refs[:4]
    refs = refs[4:]
    if not last:
        send_ref, zloc_ref, land_z_ref = refs[:3]
        refs = refs[3:]
        wide_ref, item_ref, tile_ref = refs
    else:
        wide_ref, step_tmp, resid_tmp = refs
    cap, devices, pairs = plan.cap, plan.devices, plan.pairs

    wide_ref[...] = recv_ref[...].astype(F32)
    lane = lax.broadcasted_iota(jnp.int32, (devices, LANES), 1)
    heads = [wide_ref[pl.ds(c, devices, stride=plan.zrows), :] for c in range(cap)]
    tails = [wide_ref[pl.ds(cap + c, devices, stride=plan.zrows), :] for c in range(cap)]
    scalars = (lane >= LB) & (lane < LB + 3)
    alpha = rho_ref[0:1, 0:1] / whole_sum(jnp.where(scalars, tails[0], 0.0))
    lead = bf_dot(pick_ref[...], jnp.concatenate(heads, axis=0).astype(BF16), NN)
    tail = bf_dot(pick_ref[...], jnp.concatenate(tails, axis=0).astype(BF16), NN)
    half = lower_half((pairs, LANES))
    even, odd = lead[:pairs], lead[pairs:]
    grads = [
        jnp.where(half, even, roll_half(odd)),
        jnp.where(half, roll_half(even), odd),
        jnp.where(half, tail[:pairs], roll_half(tail[pairs:])),
    ]

    parts = [ref[...].astype(F32) for ref in part_refs]
    while len(parts) > 1:
        parts = [parts[i] + parts[i + 1] for i in range(0, len(parts), 2)]
    knot_dir = knot_dir_ref[...]
    knot_q = parts[0] + knot_damp_ref[...] * knot_dir
    step = alpha * knot_dir
    knot_step_out[...] = step if first else knot_step_ref[...] + step
    knot_resid_out[...] = knot_resid_ref[...] - alpha * knot_q

    step_to, resid_to = (step_tmp, resid_tmp) if last else (land_step_out, land_resid_out)
    land = []
    for a in range(3):
        spot = pl.ds(a * pairs, pairs)
        along = land_dir_ref[spot, :]
        q = grads[a] + land_damp_ref[spot, :] * along
        step = alpha * along
        step_to[spot, :] = step if first else land_step_ref[spot, :] + step
        value = land_resid_ref[spot, :] - alpha * q
        resid_to[spot, :] = value
        land.append(value)
    if last:
        for j in range(pairs):
            cut = pl.ds(j * LANES, LANES)
            land_step_out[:, cut] = step_tmp[pl.ds(j, 3, stride=pairs), :]
            land_resid_out[:, cut] = resid_tmp[pl.ds(j, 3, stride=pairs), :]
        return
    land_z = scale_land(plan, pinv_ref, land)
    energy = jnp.zeros((pairs, LANES), F32)
    for a in range(3):
        land_z_ref[pl.ds(a * pairs, pairs), :] = land_z[a]
        energy = energy + land[a] * land_z[a]
    out, v1, v12, knot_energy, _, _ = local_sweeps(
        plan, knot_resid_out, couple_ref, dinv_ref, cuts_ref, zloc_ref
    )
    scalar = whole_sum(energy) + leader(place_ref) * whole_sum(knot_energy)
    pack_first(
        plan, plan.rw, plan.held, pick_ref, land_z, scalar, [out, v1, v12],
        place_ref, item_ref, tile_ref, send_ref,
    )


class Arrival:
    def __init__(self, ref, copy):
        self.ref, self.copy, self.shape = ref, copy, ref.shape

    def __getitem__(self, index):
        if self.copy is not None:
            self.copy.wait()
            self.copy = None
        return self.ref[index]


def call(kernel, name, outs, args, scratch):
    count, made = len(args), len(outs)

    def body(*refs):
        sources, results = refs[:count], refs[count : count + made]
        landed = refs[count + made : 2 * count + made]
        rest, sems = refs[2 * count + made : -1], refs[-1]
        arrivals = []
        for index in range(count):
            copy = pltpu.make_async_copy(sources[index], landed[index], sems.at[index])
            copy.start()
            arrivals.append(Arrival(landed[index], copy))
        place = (lax.axis_index("tm"), lax.axis_index("lm"))
        kernel(place, *arrivals, *results, *rest)
        for arrival in arrivals:
            if arrival.copy is not None:
                arrival.copy.wait()

    def block(shape):
        return pl.BlockSpec(shape, lambda step: (0,) * len(shape))

    return pl.pallas_call(
        body,
        name=name,
        grid=(1,),
        out_shape=[jax.ShapeDtypeStruct(shape, dtype) for shape, dtype in outs],
        in_specs=[pl.BlockSpec(memory_space=pl.ANY)] * count,
        out_specs=[block(shape) for shape, _ in outs],
        scratch_shapes=[pltpu.VMEM(arg.shape, arg.dtype) for arg in args]
        + scratch
        + [pltpu.SemaphoreType.DMA((count,))],
        compiler_params=pltpu.CompilerParams(vmem_limit_bytes=67_043_328),
    )(*args)


def exchange(blocks, devices):
    rows = blocks.shape[0] // devices
    shaped = blocks.reshape(devices, rows, LANES)
    moved = lax.all_to_all(shaped, AXES, split_axis=0, concat_axis=0, tiled=True)
    return moved.reshape(blocks.shape)


def swap(value, mask):
    count = lax.axis_size("lm")
    return lax.ppermute(value, "lm", [(i, i ^ mask) for i in range(count)])


def on_device(
    knot_right_side,
    land_rhs,
    jac_knot,
    jac_land,
    obs_knot,
    obs_slot,
    obs_count,
    send_list,
    couple,
    knot_dinv,
    cuts,
    land_pinv,
    knot_damp,
    land_damp,
):
    comps, knots, vehicles = knot_right_side.shape
    observed, height, knot_width = jac_knot.shape
    rows = observed * height
    cap = send_list.shape[2]
    n_tm, n_lm = lax.axis_size("tm"), lax.axis_size("lm")
    plan = Plan(
        comps, knots, land_rhs.shape[1], rows, n_tm, n_lm, cap, jac_land.shape[2]
    )
    devices, slots, field, pairs = plan.devices, plan.slots, plan.field, plan.pairs
    square = comps * comps

    resid = knot_right_side.reshape(field, vehicles)
    couple = couple.reshape(square * knots, vehicles)
    dinv = knot_dinv.reshape(square * knots, vehicles)
    knot_damp = knot_damp.reshape(field, vehicles)
    jk = jac_knot.reshape(rows, knot_width)
    jl = jac_land.reshape(rows, jac_land.shape[2])
    listed = jnp.transpose(send_list[0]).reshape(1, slots)

    live = jnp.arange(height, dtype=jnp.int32)[None, :] < obs_count[:, None]
    slot = (obs_slot % cap) * devices + obs_slot // cap
    links = jnp.stack(
        [jnp.where(live, obs_knot[:, None], -1), jnp.where(live, slot[:, None], -1)]
    ).reshape(2, rows)

    groups = vehicles // VB
    lane = jnp.arange(vehicles, dtype=jnp.int32)
    ordered = (lane % groups) * VB + lane // groups
    sel = (ordered[:, None] == lane[None, :]).astype(BF16)
    spot = jnp.arange(VB * LANES, dtype=jnp.int32)
    aim = jnp.where(spot % LANES < field, (spot % LANES) * VB + spot // LANES, -1)
    spread = (aim[:, None] == jnp.arange(knot_width, dtype=jnp.int32)[None, :]).astype(BF16)

    def items_scratch(held):
        return [
            pltpu.VMEM((held * n_lm, 8, LANES), F32),
            pltpu.VMEM((up8(comps * held), LANES), F32),
        ]

    send, zloc, onward, back, land_resid, land_z, damp, pinv, pick = call(
        functools.partial(start_kernel, plan),
        "start",
        [
            ((devices * plan.rw0, LANES), F32),
            ((field, vehicles), F32),
            ((square * knots, vehicles), F32),
            ((square * knots, vehicles), F32),
            ((3 * pairs, LANES), F32),
            ((3 * pairs, LANES), F32),
            ((3 * pairs, LANES), F32),
            ((9 * pairs, LANES), F32),
            ((plan.blocks, slots), BF16),
        ],
        [resid, land_rhs, couple, dinv, cuts, land_pinv, land_damp, listed],
        items_scratch(plan.held0),
    )
    state = None
    chain = None
    steps = None
    for turn in range(ITERS):
        first, last = turn == 0, turn == ITERS - 1
        recv = exchange(send, devices)
        args = [recv, zloc, onward, back, land_z, knot_damp, damp, jk, jl, links, sel, spread]
        outs = [
            ((devices * plan.zrows, LANES), BF16),
            ((field, vehicles), BF16),
            ((8, LANES), F32),
            ((field, vehicles), F32),
            ((3 * pairs, LANES), F32),
            ((2 * slots, LANES), F32),
        ]
        if first:
            outs.append(((n_tm * 2 * square, vehicles), F32))
        else:
            args += [chain] + list(state)
        results = call(
            functools.partial(product_kernel, first, plan),
            "product_first" if first else "product",
            outs,
            args,
            [
                pltpu.VMEM((n_tm, 8, vehicles), F32),
                pltpu.VMEM((n_tm, 8, vehicles), F32),
                pltpu.VMEM((devices * plan.zrows, LANES), F32),
            ],
        )
        send, part = results[:2]
        state = results[2:6]
        if first:
            chain = results[6]
        rho, knot_dir, land_dir, _ = state
        parts = [part] + [swap(part, mask) for mask in range(1, n_lm)]
        recv = exchange(send, devices)
        args = [recv] + parts
        args += [rho, knot_dir, land_dir, resid, land_resid, knot_damp, damp, pick]
        if not first:
            args += list(steps)
        wide = pltpu.VMEM((devices * plan.zrows, LANES), F32)
        if last:
            outs = [((field, vehicles), F32), ((3, plan.land), F32)] * 2
            scratch = [wide] + [pltpu.VMEM((3 * pairs, LANES), F32)] * 2
        else:
            args += [couple, dinv, cuts, pinv]
            outs = [((field, vehicles), F32), ((3 * pairs, LANES), F32)] * 2
            outs += [
                ((devices * plan.rw, LANES), F32),
                ((field, vehicles), F32),
                ((3 * pairs, LANES), F32),
            ]
            scratch = [wide] + items_scratch(plan.held)
        results = call(
            functools.partial(update_kernel, first, last, plan),
            "update_last" if last else "update",
            outs,
            args,
            scratch,
        )
        steps = results[:2]
        resid, land_resid = results[2:4]
        if not last:
            send, zloc, land_z = results[4:]
    shape = (comps, knots, vehicles)
    return (steps[0].reshape(shape), steps[1], resid.reshape(shape), land_resid)


def solution(mesh):
    return jax.shard_map(
        on_device,
        mesh=mesh,
        in_specs=(
            P(None, "tm", None),
            P(None, ("tm", "lm")),
            P(("tm", "lm"), None, None),
            P(("tm", "lm"), None, None),
            P(("tm", "lm")),
            P(("tm", "lm")),
            P(("tm", "lm")),
            P(("tm", "lm"), None, None),
            P(None, None, "tm", None),
            P(None, None, "tm", None),
            P("tm", None),
            P(None, None, ("tm", "lm")),
            P(None, "tm", None),
            P(None, ("tm", "lm")),
        ),
        out_specs=(
            P(None, "tm", None),
            P(None, ("tm", "lm")),
            P(None, "tm", None),
            P(None, ("tm", "lm")),
        ),
        check_vma=False,
    )
```

```python
import functools
import jax
import jax.numpy as jnp
from jax import lax
from jax.experimental import pallas as pl
from jax.experimental.pallas import tpu as pltpu
from jax.sharding import PartitionSpec as P

VB = 4
LB = 64
ITERS = 3
LANES = 128
AXES = ("tm", "lm")
F32 = jnp.float32
BF16 = jnp.bfloat16

NT = (((1,), (1,)), ((), ()))
TN = (((0,), (0,)), ((), ()))
NN = (((1,), (0,)), ((), ()))


def up8(value):
    return (value + 7) // 8 * 8


def bf_dot(left, right, dims):
    return lax.dot_general(left, right, dims, preferred_element_type=F32)


def matvec(tiles, vector):
    total = tiles[0] * vector[0:1]
    for index in range(1, len(tiles)):
        total = total + tiles[index] * vector[index : index + 1]
    return total


def whole_sum(value):
    return jnp.sum(jnp.sum(value, axis=0, keepdims=True), axis=1, keepdims=True)


class Plan:
    def __init__(self, comps, knots, land, rows, n_tm, n_lm, cap, width):
        self.comps, self.knots, self.land, self.rows = comps, knots, land, rows
        self.n_tm, self.n_lm, self.cap = n_tm, n_lm, cap
        self.devices = n_tm * n_lm
        self.slots = self.devices * cap
        self.width = width
        self.field = comps * knots
        self.pairs = land // LANES
        self.blocks = land // LB
        self.zrows = up8(2 * cap)
        self.items = 3
        self.items0 = 3 + 2 * comps
        self.held = -(-self.items // n_lm)
        self.held0 = -(-self.items0 // n_lm)
        self.rw = self.zrows + up8(comps * self.held)
        self.rw0 = self.zrows + up8(comps * self.held0)

    def item_row(self, source, item, rw):
        holder = source * self.n_lm + item % self.n_lm
        return holder * rw + self.zrows + self.comps * (item // self.n_lm)


def col_tiles(ref, plan, k):
    step = plan.comps * plan.knots
    return [
        ref[pl.ds(b * plan.knots + k, plan.comps, stride=step), :] for b in range(plan.comps)
    ]


def row_tiles(ref, plan, k):
    step = plan.comps * plan.knots
    return [
        ref[pl.ds(a * step + k, plan.comps, stride=plan.knots), :] for a in range(plan.comps)
    ]


def local_sweeps(plan, resid_ref, couple_ref, dinv_ref, cuts_ref, zloc_ref, maps=False):
    comps, knots = plan.comps, plan.knots
    lanes = couple_ref.shape[1]
    minus = cuts_ref[...].astype(F32) - 1.0
    carry = None
    basis = []
    if maps:
        rows = lax.broadcasted_iota(jnp.int32, (comps, lanes), 0)
        basis = [(rows == b).astype(F32) for b in range(comps)]
    scaled, turned, scaled_maps = [], [], []
    energy = jnp.zeros((comps, lanes), F32)
    for k in range(knots):
        value = resid_ref[pl.ds(k, comps, stride=knots), :]
        if carry is not None:
            value = value + carry
        dcol = col_tiles(dinv_ref, plan, k)
        y = matvec(dcol, value)
        scaled.append(y)
        turned.append(matvec(row_tiles(dinv_ref, plan, k), value))
        energy = energy + value * y
        lcol = col_tiles(couple_ref, plan, k)
        gate = minus[k : k + 1]
        carry = gate * matvec(lcol, value)
        if maps:
            scaled_maps.append([matvec(dcol, col) for col in basis])
            basis = [gate * matvec(lcol, col) for col in basis]
    out = carry
    total = basis
    z, u = None, None
    onward = [None] * comps
    for k in reversed(range(knots)):
        lrow = row_tiles(couple_ref, plan, k)
        gate = minus[k : k + 1]
        z = scaled[k] if z is None else scaled[k] + gate * matvec(lrow, z)
        u = turned[k] if u is None else turned[k] + gate * matvec(lrow, u)
        zloc_ref[pl.ds(k, comps, stride=knots), :] = z
        if maps:
            onward = [
                scaled_maps[k][b]
                if onward[b] is None
                else scaled_maps[k][b] + gate * matvec(lrow, onward[b])
                for b in range(comps)
            ]
    return out, z, z + u, energy, total, onward


def maps_kernel(plan, place_ref, couple_ref, cuts_ref, dinv_ref, onward_ref, back_ref):
    comps, knots = plan.comps, plan.knots
    minus = cuts_ref[...].astype(F32) - 1.0
    rows = lax.broadcasted_iota(jnp.int32, (comps, couple_ref.shape[1]), 0)
    eye = [(rows == b).astype(F32) for b in range(comps)]
    basis, scaled = eye, []
    for k in range(knots):
        dcol = col_tiles(dinv_ref, plan, k)
        scaled.append([matvec(dcol, col) for col in basis])
        if k + 1 < knots:
            lcol = col_tiles(couple_ref, plan, k)
            basis = [minus[k : k + 1] * matvec(lcol, col) for col in basis]
    onward, back = None, eye
    for k in reversed(range(knots)):
        lrow = row_tiles(couple_ref, plan, k)
        gate = minus[k : k + 1]
        back = [gate * matvec(lrow, col) for col in back]
        if onward is None:
            onward = scaled[k]
        else:
            onward = [scaled[k][b] + gate * matvec(lrow, onward[b]) for b in range(comps)]
        for b in range(comps):
            spot = pl.ds(b * knots + k, comps, stride=comps * knots)
            onward_ref[spot, :] = onward[b]
            back_ref[spot, :] = back[b]


def scale_land(plan, pinv_ref, land):
    pairs = plan.pairs
    result = []
    for a in range(3):
        total = pinv_ref[pl.ds(3 * a * pairs, pairs), :] * land[0]
        for b in range(1, 3):
            total = total + pinv_ref[pl.ds((3 * a + b) * pairs, pairs), :] * land[b]
        result.append(total)
    return result


def lower_half(shape):
    return lax.broadcasted_iota(jnp.int32, shape, 1) < LB


def roll_half(value):
    return pltpu.roll(value, LB, 1)


def split3(value):
    high = value.astype(BF16)
    rest = value - high.astype(F32)
    mid = rest.astype(BF16)
    low = (rest - mid.astype(F32)).astype(BF16)
    return high, mid, low


def pack_first(plan, rw, held, pick_ref, land_z, scalar, items, place_ref, item_ref, tile_ref, send_ref):
    devices, cap, comps = plan.devices, plan.cap, plan.comps
    half = lower_half(land_z[0].shape)
    z0, z1, z2 = land_z
    r0, r1, r2 = roll_half(z0), roll_half(z1), roll_half(z2)
    zero = jnp.zeros_like(z0)
    first = jnp.concatenate([jnp.where(half, z0, r1), jnp.where(half, r0, z1)], axis=0)
    second = jnp.concatenate([jnp.where(half, z2, zero), jnp.where(half, r2, zero)], axis=0)
    both = jnp.concatenate([first, second], axis=1)
    stacked = jnp.concatenate(list(split3(both)), axis=0)
    pick = pick_ref[...]
    picks = jnp.concatenate([pick, pick, pick], axis=0)
    rows = bf_dot(picks, stacked, TN)
    spot = lax.broadcasted_iota(jnp.int32, (devices, LANES), 1) == LB
    for c in range(cap):
        part = rows[c * devices : (c + 1) * devices]
        tail = part[:, LANES:]
        if c == 0:
            tail = jnp.where(spot, scalar, tail)
        send_ref[pl.ds(c, devices, stride=rw), :] = part[:, :LANES]
        send_ref[pl.ds(cap + c, devices, stride=rw), :] = tail
    for unused in range(2 * cap, plan.zrows):
        send_ref[pl.ds(unused, devices, stride=rw), :] = jnp.zeros((devices, LANES), F32)
    item_ref[...] = jnp.zeros_like(item_ref)
    for index, item in enumerate(items):
        item_ref[index, pl.ds(0, comps), :] = item
    tile_ref[...] = jnp.zeros_like(tile_ref)
    mine = place_ref[1]
    for k in range(held):
        tile_ref[pl.ds(comps * k, comps), :] = item_ref[k * plan.n_lm + mine, pl.ds(0, comps), :]
    tile = tile_ref[...]
    for d in range(devices):
        send_ref[pl.ds(d * rw + plan.zrows, rw - plan.zrows), :] = tile


def leader(place_ref):
    return (place_ref[1] == 0).astype(F32)


def start_kernel(
    plan,
    place_ref,
    rhs_ref,
    damp_ref,
    pinv_ref,
    list_ref,
    cuts_ref,
    resid_ref,
    dinv_ref,
    couple_ref,
    send_ref,
    zloc_ref,
    land_ref,
    land_z_ref,
    land_damp_ref,
    land_pinv_ref,
    pick_ref,
    item_ref,
    tile_ref,
):
    pairs = plan.pairs
    for j in range(pairs):
        cut = pl.ds(j * LANES, LANES)
        land_ref[pl.ds(j, 3, stride=pairs), :] = rhs_ref[:, cut]
        land_damp_ref[pl.ds(j, 3, stride=pairs), :] = damp_ref[:, cut]
        for a in range(3):
            land_pinv_ref[pl.ds(3 * a * pairs + j, 3, stride=pairs), :] = pinv_ref[a, :, cut]
    index = lax.broadcasted_iota(jnp.int32, (plan.blocks, plan.slots), 0)
    wanted = list_ref[...]
    wanted = jnp.concatenate([wanted[c : c + 1] for c in range(plan.cap)], axis=1)
    wanted = (wanted % 2) * pairs + wanted // 2
    pick_ref[...] = (index == wanted).astype(F32).astype(BF16)
    land = [land_ref[pl.ds(a * pairs, pairs), :] for a in range(3)]
    land_z = scale_land(plan, land_pinv_ref, land)
    energy = jnp.zeros((pairs, LANES), F32)
    for a in range(3):
        land_z_ref[pl.ds(a * pairs, pairs), :] = land_z[a]
        energy = energy + land[a] * land_z[a]
    out, v1, v12, knot_energy, total, inner = local_sweeps(
        plan, resid_ref, couple_ref, dinv_ref, cuts_ref, zloc_ref, True
    )
    scalar = whole_sum(energy) + leader(place_ref) * whole_sum(knot_energy)
    pack_first(
        plan, plan.rw0, plan.held0, pick_ref, land_z, scalar, [out, v1, v12] + total + inner,
        place_ref, item_ref, tile_ref, send_ref,
    )


def product_kernel(first, plan, *refs):
    refs = list(refs)
    place_ref, recv_ref = refs[:2]
    refs = refs[2:]
    rw = plan.rw0 if first else plan.rw
    if not first:
        chain_in_ref, rho_in_ref, slot_in_ref, land_in_ref, knot_in_ref = refs[:5]
        refs = refs[5:]
    land_z_ref, land_damp_ref, zloc_ref, onward_ref, back_ref = refs[:5]
    knot_damp_ref, sel_ref, spread_ref, link_ref, jl_ref, jk_ref = refs[5:11]
    outs = refs[11:]
    send_ref, part_ref, rho_ref, knot_ref, land_ref, slot_ref = outs[:6]
    outs = outs[6:]
    if first:
        chain_ref = outs[0]
        outs = outs[1:]
    else:
        chain_ref = chain_in_ref
    entry_ref, arrive_ref, wide_ref = outs
    comps, knots, cap, devices = plan.comps, plan.knots, plan.cap, plan.devices
    lanes = zloc_ref.shape[1]
    square = comps * comps

    if first:
        for s in range(plan.n_tm):
            for m in range(2 * comps):
                spot = plan.item_row(s, 3 + m, rw)
                chain_ref[pl.ds(s * 2 * square + m * comps, comps), :] = recv_ref[
                    pl.ds(spot, comps), :
                ]

    def item(s, index):
        return recv_ref[pl.ds(plan.item_row(s, index, rw), comps), :]

    incoming = None
    firsts = []
    heat = jnp.zeros((comps, lanes), F32)
    for s in range(plan.n_tm):
        base = s * 2 * square
        v1 = item(s, 1)
        if incoming is None:
            entry_ref[s, pl.ds(0, comps), :] = jnp.zeros((comps, lanes), F32)
            firsts.append(v1)
            incoming = item(s, 0)
        else:
            entry_ref[s, pl.ds(0, comps), :] = incoming
            inner = [chain_ref[pl.ds(base + square + b * comps, comps), :] for b in range(comps)]
            pushed = matvec(inner, incoming)
            heat = heat + incoming * (item(s, 2) + pushed)
            firsts.append(v1 + pushed)
            if s + 1 < plan.n_tm:
                total = [chain_ref[pl.ds(base + b * comps, comps), :] for b in range(comps)]
                incoming = matvec(total, incoming) + item(s, 0)
    arriving = None
    for s in reversed(range(plan.n_tm)):
        base = s * 2 * square
        if arriving is None:
            arrive_ref[s, pl.ds(0, comps), :] = jnp.zeros((comps, lanes), F32)
            arriving = firsts[s]
        else:
            arrive_ref[s, pl.ds(0, comps), :] = arriving
            if s > 0:
                back = [
                    chain_ref[pl.ds(base + a, comps, stride=comps), :] for a in range(comps)
                ]
                arriving = firsts[s] + matvec(back, arriving)

    lane = lax.broadcasted_iota(jnp.int32, (devices, LANES), 1)
    tails = [recv_ref[pl.ds(cap + c, devices, stride=rw), :] for c in range(cap)]
    heads = [recv_ref[pl.ds(c, devices, stride=rw), :] for c in range(cap)]
    rho = whole_sum(jnp.where(lane == LB, tails[0], 0.0)) + whole_sum(heat)
    rho_ref[...] = jnp.broadcast_to(rho, rho_ref.shape)
    if not first:
        beta = rho / rho_in_ref[0:1, 0:1]
    half = lane < LB
    tails = [jnp.where(half, tail, 0.0) for tail in tails]
    slot_dir = []
    for index, rows in enumerate(heads + tails):
        spot = pl.ds(index * devices, devices)
        if not first:
            rows = rows + beta * slot_in_ref[spot, :]
        slot_ref[spot, :] = rows
        slot_dir.append(rows)
    land_dir = land_z_ref[...]
    if not first:
        land_dir = land_dir + beta * land_in_ref[...]
    land_ref[...] = land_dir
    heat = whole_sum(land_damp_ref[...] * land_dir * land_dir)

    mine = place_ref[0]
    entry = entry_ref[mine, pl.ds(0, comps), :]
    arrive = arrive_ref[mine, pl.ds(0, comps), :]
    for a in range(comps):
        total = zloc_ref[pl.ds(a * knots, knots), :]
        for b in range(comps):
            spot = pl.ds((a * comps + b) * knots, knots)
            total = total + onward_ref[spot, :] * entry[b : b + 1]
            total = total + back_ref[spot, :] * arrive[b : b + 1]
        if not first:
            total = total + beta * knot_in_ref[pl.ds(a * knots, knots), :]
        knot_ref[pl.ds(a * knots, knots), :] = total
    knot_dir = knot_ref[...]
    heat = heat + leader(place_ref) * whole_sum(knot_damp_ref[...] * knot_dir * knot_dir)

    groups = lanes // VB
    narrow = knot_dir.astype(BF16)
    padded = jnp.concatenate([narrow, jnp.zeros((LANES - plan.field, lanes), BF16)], axis=0)
    turned = bf_dot(sel_ref[...], padded, NT).astype(BF16)
    joined = jnp.concatenate(
        [turned[i * groups : (i + 1) * groups] for i in range(VB)], axis=1
    )
    knot_rows = bf_dot(joined, spread_ref[...], NN).astype(BF16)
    slot_rows = jnp.concatenate(
        [
            jnp.concatenate(slot_dir[:cap], axis=0).astype(BF16),
            jnp.concatenate(slot_dir[cap:], axis=0).astype(BF16)[:, :LB],
        ],
        axis=1,
    )
    chunk = 512
    knot_total, land_total = None, None
    for start in range(0, plan.rows, chunk):
        cut = pl.ds(start, chunk)
        jk, jl = jk_ref[cut, :], jl_ref[cut, :]
        near = bf_dot(knot_rows, jk, NT)
        far = bf_dot(slot_rows, jl, NT)
        knot_hit = lax.broadcasted_iota(jnp.int32, near.shape, 0) == link_ref[0:1, cut]
        slot_hit = lax.broadcasted_iota(jnp.int32, far.shape, 0) == link_ref[1:2, cut]
        resid = jnp.sum(jnp.where(knot_hit, near, 0.0), axis=0, keepdims=True) + jnp.sum(
            jnp.where(slot_hit, far, 0.0), axis=0, keepdims=True
        )
        knot_side = jnp.where(knot_hit, resid, 0.0).astype(BF16)
        slot_side = jnp.where(slot_hit, resid, 0.0).astype(BF16)
        knot_term = bf_dot(knot_side, jk, NN)
        land_term = bf_dot(slot_side, jl, NN)
        knot_total = knot_term if knot_total is None else knot_total + knot_term
        land_total = land_term if land_total is None else land_total + land_term

    parted = bf_dot(knot_total.astype(BF16), spread_ref[...], NT).astype(BF16)
    piled = jnp.concatenate(
        [parted[:, i * LANES : (i + 1) * LANES] for i in range(VB)], axis=0
    )
    part = bf_dot(piled, sel_ref[...], TN)[: plan.field]
    part_ref[...] = part.astype(BF16)
    heat = heat + whole_sum(part * knot_dir)
    land_total = land_total.astype(BF16).astype(F32)
    lead_rows = land_total[:, :LANES]
    tail_rows = jnp.concatenate(
        [land_total[:, LANES:], jnp.zeros((plan.slots, LANES - LB), F32)], axis=1
    )
    sums = jnp.zeros((devices, LANES), F32)
    for c in range(cap):
        cut = slice(c * devices, (c + 1) * devices)
        sums = sums + lead_rows[cut] * slot_dir[c] + tail_rows[cut] * slot_dir[cap + c]
    heat = heat + whole_sum(sums)
    high, mid, low = [piece.astype(F32) for piece in split3(heat)]
    if 2 * cap < plan.zrows:
        wide_ref[...] = jnp.zeros_like(wide_ref)
    for c in range(cap):
        cut = slice(c * devices, (c + 1) * devices)
        tail = tail_rows[cut]
        if c == 0:
            tail = jnp.where(lane == LB, high, tail)
            tail = jnp.where(lane == LB + 1, mid, tail)
            tail = jnp.where(lane == LB + 2, low, tail)
        wide_ref[pl.ds(c, devices, stride=plan.zrows), :] = lead_rows[cut]
        wide_ref[pl.ds(cap + c, devices, stride=plan.zrows), :] = tail
    send_ref[...] = wide_ref[...].astype(BF16)


def update_kernel(first, last, plan, *refs):
    refs = list(refs)
    place_ref = refs[0]
    refs = refs[1:]
    rho_ref, knot_dir_ref, land_dir_ref, knot_resid_ref, land_resid_ref = refs[:5]
    knot_damp_ref, land_damp_ref, pick_ref = refs[5:8]
    refs = refs[8:]
    if not first:
        knot_step_ref, land_step_ref = refs[:2]
        refs = refs[2:]
    if not last:
        couple_ref, dinv_ref, cuts_ref, pinv_ref = refs[:4]
        refs = refs[4:]
    part_refs, recv_ref = refs[: plan.n_lm], refs[plan.n_lm]
    refs = refs[plan.n_lm + 1 :]
    knot_step_out, land_step_out, knot_resid_out, land_resid_out = refs[:4]
    refs = refs[4:]
    if not last:
        send_ref, zloc_ref, land_z_ref = refs[:3]
        refs = refs[3:]
        wide_ref, item_ref, tile_ref = refs
    else:
        wide_ref, step_tmp, resid_tmp = refs
    cap, devices, pairs = plan.cap, plan.devices, plan.pairs

    wide_ref[...] = recv_ref[...].astype(F32)
    lane = lax.broadcasted_iota(jnp.int32, (devices, LANES), 1)
    heads = [wide_ref[pl.ds(c, devices, stride=plan.zrows), :] for c in range(cap)]
    tails = [wide_ref[pl.ds(cap + c, devices, stride=plan.zrows), :] for c in range(cap)]
    scalars = (lane >= LB) & (lane < LB + 3)
    alpha = rho_ref[0:1, 0:1] / whole_sum(jnp.where(scalars, tails[0], 0.0))
    lead = bf_dot(pick_ref[...], jnp.concatenate(heads, axis=0).astype(BF16), NN)
    tail = bf_dot(pick_ref[...], jnp.concatenate(tails, axis=0).astype(BF16), NN)
    half = lower_half((pairs, LANES))
    even, odd = lead[:pairs], lead[pairs:]
    grads = [
        jnp.where(half, even, roll_half(odd)),
        jnp.where(half, roll_half(even), odd),
        jnp.where(half, tail[:pairs], roll_half(tail[pairs:])),
    ]

    parts = [ref[...].astype(F32) for ref in part_refs]
    while len(parts) > 1:
        parts = [parts[i] + parts[i + 1] for i in range(0, len(parts), 2)]
    knot_dir = knot_dir_ref[...]
    knot_q = parts[0] + knot_damp_ref[...] * knot_dir
    step = alpha * knot_dir
    knot_step_out[...] = step if first else knot_step_ref[...] + step
    knot_resid_out[...] = knot_resid_ref[...] - alpha * knot_q

    step_to, resid_to = (step_tmp, resid_tmp) if last else (land_step_out, land_resid_out)
    land = []
    for a in range(3):
        spot = pl.ds(a * pairs, pairs)
        along = land_dir_ref[spot, :]
        q = grads[a] + land_damp_ref[spot, :] * along
        step = alpha * along
        step_to[spot, :] = step if first else land_step_ref[spot, :] + step
        value = land_resid_ref[spot, :] - alpha * q
        resid_to[spot, :] = value
        land.append(value)
    if last:
        for j in range(pairs):
            cut = pl.ds(j * LANES, LANES)
            land_step_out[:, cut] = step_tmp[pl.ds(j, 3, stride=pairs), :]
            land_resid_out[:, cut] = resid_tmp[pl.ds(j, 3, stride=pairs), :]
        return
    land_z = scale_land(plan, pinv_ref, land)
    energy = jnp.zeros((pairs, LANES), F32)
    for a in range(3):
        land_z_ref[pl.ds(a * pairs, pairs), :] = land_z[a]
        energy = energy + land[a] * land_z[a]
    out, v1, v12, knot_energy, _, _ = local_sweeps(
        plan, knot_resid_out, couple_ref, dinv_ref, cuts_ref, zloc_ref
    )
    scalar = whole_sum(energy) + leader(place_ref) * whole_sum(knot_energy)
    pack_first(
        plan, plan.rw, plan.held, pick_ref, land_z, scalar, [out, v1, v12],
        place_ref, item_ref, tile_ref, send_ref,
    )


class Arrival:
    def __init__(self, ref, copy):
        self.ref, self.copy, self.shape = ref, copy, ref.shape

    def __getitem__(self, index):
        if self.copy is not None:
            self.copy.wait()
            self.copy = None
        return self.ref[index]


def call(kernel, name, outs, args, scratch, loose=0, held=0):
    count, made = len(args) - held, len(outs)

    def body(*refs):
        sources, refs = refs[:count], refs[count:]
        kept, refs = refs[:held], refs[held:]
        results, refs = refs[:made], refs[made:]
        landed, rest, sems = refs[:count], refs[count:-1], refs[-1]
        arrivals = []
        for index in range(count):
            copy = pltpu.make_async_copy(sources[index], landed[index], sems.at[index])
            copy.start()
            arrivals.append(Arrival(landed[index], copy))
        place = (lax.axis_index("tm"), lax.axis_index("lm"))
        kernel(place, *arrivals, *kept, *results, *rest)
        for arrival in arrivals:
            if arrival.copy is not None:
                arrival.copy.wait()

    args = [
        pltpu.with_memory_space_constraint(arg, pltpu.HBM) if loose <= index < count else arg
        for index, arg in enumerate(args)
    ]

    def block(shape):
        return pl.BlockSpec(shape, lambda step: (0,) * len(shape))

    return pl.pallas_call(
        body,
        name=name,
        grid=(1,),
        out_shape=[pltpu.HBM(shape, dtype) for shape, dtype in outs],
        in_specs=[pl.BlockSpec(memory_space=pl.ANY)] * loose
        + [pl.BlockSpec(memory_space=pltpu.HBM)] * (count - loose)
        + [pl.BlockSpec(memory_space=pltpu.VMEM)] * held,
        out_specs=[block(shape) for shape, _ in outs],
        scratch_shapes=[pltpu.VMEM(arg.shape, arg.dtype) for arg in args[:count]]
        + scratch
        + [pltpu.SemaphoreType.DMA((count,))],
        compiler_params=pltpu.CompilerParams(vmem_limit_bytes=24 << 20),
    )(*args)


def exchange(blocks, devices):
    rows = blocks.shape[0] // devices
    shaped = blocks.reshape(devices, rows, LANES)
    moved = lax.all_to_all(shaped, AXES, split_axis=0, concat_axis=0, tiled=True)
    return moved.reshape(blocks.shape)


def swap(value, mask):
    count = lax.axis_size("lm")
    return lax.ppermute(value, "lm", [(i, i ^ mask) for i in range(count)])


def on_device(
    knot_right_side,
    land_rhs,
    jac_knot,
    jac_land,
    obs_knot,
    obs_slot,
    obs_count,
    send_list,
    couple,
    knot_dinv,
    cuts,
    land_pinv,
    knot_damp,
    land_damp,
):
    comps, knots, vehicles = knot_right_side.shape
    observed, height, knot_width = jac_knot.shape
    rows = observed * height
    cap = send_list.shape[2]
    n_tm, n_lm = lax.axis_size("tm"), lax.axis_size("lm")
    plan = Plan(
        comps, knots, land_rhs.shape[1], rows, n_tm, n_lm, cap, jac_land.shape[2]
    )
    devices, slots, field, pairs = plan.devices, plan.slots, plan.field, plan.pairs
    square = comps * comps

    resid = knot_right_side.reshape(field, vehicles)
    couple = couple.reshape(square * knots, vehicles)
    dinv = knot_dinv.reshape(square * knots, vehicles)
    knot_damp = knot_damp.reshape(field, vehicles)
    jk = jac_knot.reshape(rows, knot_width)
    jl = jac_land.reshape(rows, jac_land.shape[2])
    listed = jnp.transpose(send_list[0])

    live = jnp.arange(height, dtype=jnp.int32)[None, :] < obs_count[:, None]
    slot = (obs_slot % cap) * devices + obs_slot // cap
    links = jnp.stack(
        [jnp.where(live, obs_knot[:, None], -1), jnp.where(live, slot[:, None], -1)]
    ).reshape(2, rows)

    groups = vehicles // VB
    lane = jnp.arange(vehicles, dtype=jnp.int32)
    ordered = (lane % groups) * VB + lane // groups
    sel = (ordered[:, None] == lane[None, :]).astype(BF16)
    spot = jnp.arange(VB * LANES, dtype=jnp.int32)
    aim = jnp.where(spot % LANES < field, (spot % LANES) * VB + spot // LANES, -1)
    spread = (aim[:, None] == jnp.arange(knot_width, dtype=jnp.int32)[None, :]).astype(BF16)

    def items_scratch(held):
        return [
            pltpu.VMEM((held * n_lm, 8, LANES), F32),
            pltpu.VMEM((up8(comps * held), LANES), F32),
        ]

    send, zloc, land_resid, land_z, damp, pinv, pick = call(
        functools.partial(start_kernel, plan),
        "start",
        [
            ((devices * plan.rw0, LANES), F32),
            ((field, vehicles), F32),
            ((3 * pairs, LANES), F32),
            ((3 * pairs, LANES), F32),
            ((3 * pairs, LANES), F32),
            ((9 * pairs, LANES), F32),
            ((plan.blocks, slots), BF16),
        ],
        [land_rhs, land_damp, land_pinv, listed, cuts, resid, dinv, couple],
        items_scratch(plan.held0),
    )
    onward, back = call(
        functools.partial(maps_kernel, plan),
        "maps",
        [((square * knots, vehicles), F32)] * 2,
        [couple, cuts, dinv],
        [],
    )
    state = None
    chain = None
    steps = None
    for turn in range(ITERS):
        first, last = turn == 0, turn == ITERS - 1
        recv = exchange(send, devices)
        args = [recv]
        if not first:
            rho, knot_dir, land_dir, slot_dir = state
            args += [chain, rho, slot_dir, land_dir, knot_dir]
        args += [land_z, damp, zloc, onward, back, knot_damp, sel, spread, links, jl, jk]
        outs = [
            ((devices * plan.zrows, LANES), BF16),
            ((field, vehicles), BF16),
            ((8, LANES), F32),
            ((field, vehicles), F32),
            ((3 * pairs, LANES), F32),
            ((2 * slots, LANES), F32),
        ]
        if first:
            outs.append(((n_tm * 2 * square, vehicles), F32))
        results = call(
            functools.partial(product_kernel, first, plan),
            "product_first" if first else "product",
            outs,
            args,
            [
                pltpu.VMEM((n_tm, 8, vehicles), F32),
                pltpu.VMEM((n_tm, 8, vehicles), F32),
                pltpu.VMEM((devices * plan.zrows, LANES), F32),
            ],
            loose=1,
            held=1 if first else 2,
        )
        send, part = results[:2]
        state = results[2:6]
        if first:
            chain = results[6]
        rho, knot_dir, land_dir, _ = state
        parts = [part] + [swap(part, mask) for mask in range(1, n_lm)]
        recv = exchange(send, devices)
        args = [rho, knot_dir, land_dir, resid, land_resid, knot_damp, damp, pick]
        if not first:
            args += list(steps)
        wide = pltpu.VMEM((devices * plan.zrows, LANES), F32)
        if not last:
            args += [couple, dinv, cuts, pinv]
        args += parts + [recv]
        if last:
            outs = [((field, vehicles), F32), ((3, plan.land), F32)] * 2
            scratch = [wide] + [pltpu.VMEM((3 * pairs, LANES), F32)] * 2
        else:
            outs = [((field, vehicles), F32), ((3 * pairs, LANES), F32)] * 2
            outs += [
                ((devices * plan.rw, LANES), F32),
                ((field, vehicles), F32),
                ((3 * pairs, LANES), F32),
            ]
            scratch = [wide] + items_scratch(plan.held)
        results = call(
            functools.partial(update_kernel, first, last, plan),
            "update_last" if last else "update",
            outs,
            args,
            scratch,
            held=n_lm,
        )
        steps = results[:2]
        resid, land_resid = results[2:4]
        if not last:
            send, zloc, land_z = results[4:]
    shape = (comps, knots, vehicles)
    return (steps[0].reshape(shape), steps[1], resid.reshape(shape), land_resid)


def solution(mesh):
    return jax.shard_map(
        on_device,
        mesh=mesh,
        in_specs=(
            P(None, "tm", None),
            P(None, ("tm", "lm")),
            P(("tm", "lm"), None, None),
            P(("tm", "lm"), None, None),
            P(("tm", "lm")),
            P(("tm", "lm")),
            P(("tm", "lm")),
            P(("tm", "lm"), None, None),
            P(None, None, "tm", None),
            P(None, None, "tm", None),
            P("tm", None),
            P(None, None, ("tm", "lm")),
            P(None, "tm", None),
            P(None, ("tm", "lm")),
        ),
        out_specs=(
            P(None, "tm", None),
            P(None, ("tm", "lm")),
            P(None, "tm", None),
            P(None, ("tm", "lm")),
        ),
        check_vma=False,
    )
```

```python
import functools
import jax
import jax.numpy as jnp
from jax import lax
from jax.experimental import pallas as pl
from jax.experimental.pallas import tpu as pltpu
from jax.sharding import PartitionSpec as P

VB = 4
LB = 64
ITERS = 3
LANES = 128
AXES = ("tm", "lm")
F32 = jnp.float32
BF16 = jnp.bfloat16

NT = (((1,), (1,)), ((), ()))
TN = (((0,), (0,)), ((), ()))
NN = (((1,), (0,)), ((), ()))


def up8(value):
    return (value + 7) // 8 * 8


def bf_dot(left, right, dims):
    return lax.dot_general(left, right, dims, preferred_element_type=F32)


def matvec(tiles, vector):
    total = tiles[0] * vector[0:1]
    for index in range(1, len(tiles)):
        total = total + tiles[index] * vector[index : index + 1]
    return total


def whole_sum(value):
    return jnp.sum(jnp.sum(value, axis=0, keepdims=True), axis=1, keepdims=True)


class Plan:
    def __init__(self, comps, knots, land, rows, n_tm, n_lm, cap, width):
        self.comps, self.knots, self.land, self.rows = comps, knots, land, rows
        self.n_tm, self.n_lm, self.cap = n_tm, n_lm, cap
        self.devices = n_tm * n_lm
        self.slots = self.devices * cap
        self.width = width
        self.field = comps * knots
        self.pairs = land // LANES
        self.blocks = land // LB
        self.zrows = up8(2 * cap)
        self.items0 = 3 + 2 * comps
        self.held0 = -(-self.items0 // n_lm)
        self.rw0 = self.zrows + up8(comps * self.held0)
        self.per = -(-5 * comps // n_lm)
        self.rw = self.zrows + up8(self.per)

    def item_row(self, source, item):
        holder = source * self.n_lm + item % self.n_lm
        return holder * self.rw0 + self.zrows + self.comps * (item // self.n_lm)


def col_tiles(ref, plan, k):
    step = plan.comps * plan.knots
    return [
        ref[pl.ds(b * plan.knots + k, plan.comps, stride=step), :] for b in range(plan.comps)
    ]


def row_tiles(ref, plan, k):
    step = plan.comps * plan.knots
    return [
        ref[pl.ds(a * step + k, plan.comps, stride=plan.knots), :] for a in range(plan.comps)
    ]


def local_sweeps(plan, resid_ref, couple_ref, dinv_ref, cuts_ref, zloc_ref, maps=False):
    comps, knots = plan.comps, plan.knots
    lanes = couple_ref.shape[1]
    minus = cuts_ref[...].astype(F32) - 1.0
    carry = None
    basis = []
    if maps:
        rows = lax.broadcasted_iota(jnp.int32, (comps, lanes), 0)
        basis = [(rows == b).astype(F32) for b in range(comps)]
    scaled, turned, scaled_maps = [], [], []
    energy = jnp.zeros((comps, lanes), F32)
    for k in range(knots):
        value = resid_ref[pl.ds(k, comps, stride=knots), :]
        if carry is not None:
            value = value + carry
        dcol = col_tiles(dinv_ref, plan, k)
        y = matvec(dcol, value)
        scaled.append(y)
        turned.append(matvec(row_tiles(dinv_ref, plan, k), value))
        energy = energy + value * y
        lcol = col_tiles(couple_ref, plan, k)
        gate = minus[k : k + 1]
        carry = gate * matvec(lcol, value)
        if maps:
            scaled_maps.append([matvec(dcol, col) for col in basis])
            basis = [gate * matvec(lcol, col) for col in basis]
    out = carry
    total = basis
    z, u = None, None
    onward = [None] * comps
    for k in reversed(range(knots)):
        lrow = row_tiles(couple_ref, plan, k)
        gate = minus[k : k + 1]
        z = scaled[k] if z is None else scaled[k] + gate * matvec(lrow, z)
        u = turned[k] if u is None else turned[k] + gate * matvec(lrow, u)
        zloc_ref[pl.ds(k, comps, stride=knots), :] = z
        if maps:
            onward = [
                scaled_maps[k][b]
                if onward[b] is None
                else scaled_maps[k][b] + gate * matvec(lrow, onward[b])
                for b in range(comps)
            ]
    return out, z, z + u, energy, total, onward


def maps_kernel(plan, place_ref, couple_ref, cuts_ref, dinv_ref, onward_ref, back_ref):
    comps, knots = plan.comps, plan.knots
    minus = cuts_ref[...].astype(F32) - 1.0
    rows = lax.broadcasted_iota(jnp.int32, (comps, couple_ref.shape[1]), 0)
    eye = [(rows == b).astype(F32) for b in range(comps)]
    basis, scaled = eye, []
    for k in range(knots):
        dcol = col_tiles(dinv_ref, plan, k)
        scaled.append([matvec(dcol, col) for col in basis])
        if k + 1 < knots:
            lcol = col_tiles(couple_ref, plan, k)
            basis = [minus[k : k + 1] * matvec(lcol, col) for col in basis]
    onward, back = None, eye
    for k in reversed(range(knots)):
        lrow = row_tiles(couple_ref, plan, k)
        gate = minus[k : k + 1]
        back = [gate * matvec(lrow, col) for col in back]
        if onward is None:
            onward = scaled[k]
        else:
            onward = [scaled[k][b] + gate * matvec(lrow, onward[b]) for b in range(comps)]
        for b in range(comps):
            spot = pl.ds(b * knots + k, comps, stride=comps * knots)
            onward_ref[spot, :] = onward[b]
            back_ref[spot, :] = back[b]


def scale_land(plan, pinv_ref, land):
    pairs = plan.pairs
    result = []
    for a in range(3):
        total = pinv_ref[pl.ds(3 * a * pairs, pairs), :] * land[0]
        for b in range(1, 3):
            total = total + pinv_ref[pl.ds((3 * a + b) * pairs, pairs), :] * land[b]
        result.append(total)
    return result


def lower_half(shape):
    return lax.broadcasted_iota(jnp.int32, shape, 1) < LB


def roll_half(value):
    return pltpu.roll(value, LB, 1)


def split3(value):
    high = value.astype(BF16)
    rest = value - high.astype(F32)
    mid = rest.astype(BF16)
    low = (rest - mid.astype(F32)).astype(BF16)
    return high, mid, low


def land_blocks(land_z):
    half = lower_half(land_z[0].shape)
    z0, z1, z2 = land_z
    r0, r1, r2 = roll_half(z0), roll_half(z1), roll_half(z2)
    zero = jnp.zeros_like(z0)
    first = jnp.concatenate([jnp.where(half, z0, r1), jnp.where(half, r0, z1)], axis=0)
    second = jnp.concatenate([jnp.where(half, z2, zero), jnp.where(half, r2, zero)], axis=0)
    return jnp.concatenate([first, second], axis=1)


def place_land(plan, rw, rows, marks, stage_ref):
    devices, cap = plan.devices, plan.cap
    lane = lax.broadcasted_iota(jnp.int32, (devices, LANES), 1)
    for c in range(cap):
        part = rows[c * devices : (c + 1) * devices]
        tail = part[:, LANES:]
        if c == 0:
            for index, mark in enumerate(marks):
                tail = jnp.where(lane == LB + index, mark, tail)
        stage_ref[pl.ds(c, devices, stride=rw), :] = part[:, :LANES]
        stage_ref[pl.ds(cap + c, devices, stride=rw), :] = tail
    for unused in range(2 * cap, plan.zrows):
        stage_ref[pl.ds(unused, devices, stride=rw), :] = jnp.zeros((devices, LANES), F32)


def pack_wide(plan, pick_ref, land_z, scalar, items, place_ref, item_ref, tile_ref, send_ref):
    rw, comps = plan.rw0, plan.comps
    stacked = jnp.concatenate(list(split3(land_blocks(land_z))), axis=0)
    pick = pick_ref[...]
    rows = bf_dot(jnp.concatenate([pick, pick, pick], axis=0), stacked, TN)
    place_land(plan, rw, rows, [scalar], send_ref)
    item_ref[...] = jnp.zeros_like(item_ref)
    for index, item in enumerate(items):
        item_ref[index, pl.ds(0, comps), :] = item
    tile_ref[...] = jnp.zeros_like(tile_ref)
    mine = place_ref[1]
    for k in range(plan.held0):
        tile_ref[pl.ds(comps * k, comps), :] = item_ref[k * plan.n_lm + mine, pl.ds(0, comps), :]
    tile = tile_ref[...]
    for d in range(plan.devices):
        send_ref[pl.ds(d * rw + plan.zrows, rw - plan.zrows), :] = tile


def pack_narrow(plan, pick_ref, land_z, scalar, items, place_ref, item_ref, stage_ref, send_ref):
    rw, comps, per = plan.rw, plan.comps, plan.per
    rows = bf_dot(pick_ref[...], land_blocks(land_z).astype(BF16), TN)
    place_land(plan, rw, rows, [piece.astype(F32) for piece in split3(scalar)], stage_ref)
    out, v1, v12 = items
    pieces = []
    for item in (out, v1):
        high, low, _ = split3(item)
        pieces += [high.astype(F32), low.astype(F32)]
    pieces.append(v12)
    item_ref[...] = jnp.zeros_like(item_ref)
    for index, piece in enumerate(pieces):
        begin = 0
        while begin < comps:
            flat = comps * index + begin
            run = min(comps - begin, per - flat % per)
            item_ref[flat // per, pl.ds(flat % per, run), :] = piece[begin : begin + run]
            begin += run
    tile = item_ref[place_ref[1]]
    for d in range(plan.devices):
        stage_ref[pl.ds(d * rw + plan.zrows, rw - plan.zrows), :] = tile
    send_ref[...] = stage_ref[...].astype(BF16)


def leader(place_ref):
    return (place_ref[1] == 0).astype(F32)


def start_kernel(
    plan,
    place_ref,
    rhs_ref,
    damp_ref,
    pinv_ref,
    list_ref,
    cuts_ref,
    resid_ref,
    dinv_ref,
    couple_ref,
    send_ref,
    zloc_ref,
    land_ref,
    land_z_ref,
    land_damp_ref,
    land_pinv_ref,
    pick_ref,
    item_ref,
    tile_ref,
):
    pairs = plan.pairs
    for j in range(pairs):
        cut = pl.ds(j * LANES, LANES)
        land_ref[pl.ds(j, 3, stride=pairs), :] = rhs_ref[:, cut]
        land_damp_ref[pl.ds(j, 3, stride=pairs), :] = damp_ref[:, cut]
        for a in range(3):
            land_pinv_ref[pl.ds(3 * a * pairs + j, 3, stride=pairs), :] = pinv_ref[a, :, cut]
    index = lax.broadcasted_iota(jnp.int32, (plan.blocks, plan.slots), 0)
    wanted = list_ref[...]
    wanted = jnp.concatenate([wanted[c : c + 1] for c in range(plan.cap)], axis=1)
    wanted = (wanted % 2) * pairs + wanted // 2
    pick_ref[...] = (index == wanted).astype(F32).astype(BF16)
    land = [land_ref[pl.ds(a * pairs, pairs), :] for a in range(3)]
    land_z = scale_land(plan, land_pinv_ref, land)
    energy = jnp.zeros((pairs, LANES), F32)
    for a in range(3):
        land_z_ref[pl.ds(a * pairs, pairs), :] = land_z[a]
        energy = energy + land[a] * land_z[a]
    out, v1, v12, knot_energy, total, inner = local_sweeps(
        plan, resid_ref, couple_ref, dinv_ref, cuts_ref, zloc_ref, True
    )
    scalar = whole_sum(energy) + leader(place_ref) * whole_sum(knot_energy)
    pack_wide(
        plan, pick_ref, land_z, scalar, [out, v1, v12] + total + inner,
        place_ref, item_ref, tile_ref, send_ref,
    )


def product_kernel(first, plan, *refs):
    refs = list(refs)
    place_ref, recv_ref = refs[:2]
    refs = refs[2:]
    rw = plan.rw0 if first else plan.rw
    if not first:
        chain_in_ref, rho_in_ref, slot_in_ref, land_in_ref, knot_in_ref = refs[:5]
        refs = refs[5:]
    land_z_ref, land_damp_ref, zloc_ref, onward_ref, back_ref = refs[:5]
    knot_damp_ref, sel_ref, spread_ref, link_ref, jl_ref, jk_ref = refs[5:11]
    outs = refs[11:]
    send_ref, part_ref, rho_ref, knot_ref, land_ref, slot_ref = outs[:6]
    outs = outs[6:]
    if first:
        chain_ref = outs[0]
        outs = outs[1:]
    else:
        chain_ref = chain_in_ref
    entry_ref, arrive_ref, wide_ref = outs[:3]
    outs = outs[3:]
    comps, knots, cap, devices = plan.comps, plan.knots, plan.cap, plan.devices
    lanes = zloc_ref.shape[1]
    square = comps * comps

    if first:
        for s in range(plan.n_tm):
            for m in range(2 * comps):
                spot = plan.item_row(s, 3 + m)
                chain_ref[pl.ds(s * 2 * square + m * comps, comps), :] = recv_ref[
                    pl.ds(spot, comps), :
                ]

        def item(s, index):
            return recv_ref[pl.ds(plan.item_row(s, index), comps), :]

    else:
        got_ref, flat_ref = outs
        got_ref[...] = recv_ref[...].astype(F32)
        recv_ref = got_ref
        per = plan.per
        for d in range(devices):
            flat_ref[pl.ds(d * per, per), :] = got_ref[pl.ds(d * rw + plan.zrows, per), :]

        def item(s, index):
            base = s * plan.n_lm * per
            if index == 2:
                return flat_ref[pl.ds(base + 4 * comps, comps), :]
            begin = base + 2 * index * comps
            high = flat_ref[pl.ds(begin, comps), :]
            return high + flat_ref[pl.ds(begin + comps, comps), :]

    incoming = None
    firsts = []
    heat = jnp.zeros((comps, lanes), F32)
    for s in range(plan.n_tm):
        base = s * 2 * square
        v1 = item(s, 1)
        if incoming is None:
            entry_ref[s, pl.ds(0, comps), :] = jnp.zeros((comps, lanes), F32)
            firsts.append(v1)
            incoming = item(s, 0)
        else:
            entry_ref[s, pl.ds(0, comps), :] = incoming
            inner = [chain_ref[pl.ds(base + square + b * comps, comps), :] for b in range(comps)]
            pushed = matvec(inner, incoming)
            heat = heat + incoming * (item(s, 2) + pushed)
            firsts.append(v1 + pushed)
            if s + 1 < plan.n_tm:
                total = [chain_ref[pl.ds(base + b * comps, comps), :] for b in range(comps)]
                incoming = matvec(total, incoming) + item(s, 0)
    arriving = None
    for s in reversed(range(plan.n_tm)):
        base = s * 2 * square
        if arriving is None:
            arrive_ref[s, pl.ds(0, comps), :] = jnp.zeros((comps, lanes), F32)
            arriving = firsts[s]
        else:
            arrive_ref[s, pl.ds(0, comps), :] = arriving
            if s > 0:
                back = [
                    chain_ref[pl.ds(base + a, comps, stride=comps), :] for a in range(comps)
                ]
                arriving = firsts[s] + matvec(back, arriving)

    lane = lax.broadcasted_iota(jnp.int32, (devices, LANES), 1)
    tails = [recv_ref[pl.ds(cap + c, devices, stride=rw), :] for c in range(cap)]
    heads = [recv_ref[pl.ds(c, devices, stride=rw), :] for c in range(cap)]
    marked = (lane >= LB) & (lane < LB + (1 if first else 3))
    rho = whole_sum(jnp.where(marked, tails[0], 0.0)) + whole_sum(heat)
    rho_ref[...] = jnp.broadcast_to(rho, rho_ref.shape)
    if not first:
        beta = rho / rho_in_ref[0:1, 0:1]
    half = lane < LB
    tails = [jnp.where(half, tail, 0.0) for tail in tails]
    slot_dir = []
    for index, rows in enumerate(heads + tails):
        spot = pl.ds(index * devices, devices)
        if not first:
            rows = rows + beta * slot_in_ref[spot, :]
        slot_ref[spot, :] = rows
        slot_dir.append(rows)
    land_dir = land_z_ref[...]
    if not first:
        land_dir = land_dir + beta * land_in_ref[...]
    land_ref[...] = land_dir
    heat = whole_sum(land_damp_ref[...] * land_dir * land_dir)

    mine = place_ref[0]
    entry = entry_ref[mine, pl.ds(0, comps), :]
    arrive = arrive_ref[mine, pl.ds(0, comps), :]
    for a in range(comps):
        total = zloc_ref[pl.ds(a * knots, knots), :]
        for b in range(comps):
            spot = pl.ds((a * comps + b) * knots, knots)
            total = total + onward_ref[spot, :] * entry[b : b + 1]
            total = total + back_ref[spot, :] * arrive[b : b + 1]
        if not first:
            total = total + beta * knot_in_ref[pl.ds(a * knots, knots), :]
        knot_ref[pl.ds(a * knots, knots), :] = total
    knot_dir = knot_ref[...]
    heat = heat + leader(place_ref) * whole_sum(knot_damp_ref[...] * knot_dir * knot_dir)

    groups = lanes // VB
    narrow = knot_dir.astype(BF16)
    padded = jnp.concatenate([narrow, jnp.zeros((LANES - plan.field, lanes), BF16)], axis=0)
    turned = bf_dot(sel_ref[...], padded, NT).astype(BF16)
    joined = jnp.concatenate(
        [turned[i * groups : (i + 1) * groups] for i in range(VB)], axis=1
    )
    knot_rows = bf_dot(joined, spread_ref[...], NN).astype(BF16)
    slot_rows = jnp.concatenate(
        [
            jnp.concatenate(slot_dir[:cap], axis=0).astype(BF16),
            jnp.concatenate(slot_dir[cap:], axis=0).astype(BF16)[:, :LB],
        ],
        axis=1,
    )
    chunk = 512
    knot_total, land_total = None, None
    for start in range(0, plan.rows, chunk):
        cut = pl.ds(start, chunk)
        jk, jl = jk_ref[cut, :], jl_ref[cut, :]
        near = bf_dot(knot_rows, jk, NT)
        far = bf_dot(slot_rows, jl, NT)
        knot_hit = lax.broadcasted_iota(jnp.int32, near.shape, 0) == link_ref[0:1, cut]
        slot_hit = lax.broadcasted_iota(jnp.int32, far.shape, 0) == link_ref[1:2, cut]
        resid = jnp.sum(jnp.where(knot_hit, near, 0.0), axis=0, keepdims=True) + jnp.sum(
            jnp.where(slot_hit, far, 0.0), axis=0, keepdims=True
        )
        knot_side = jnp.where(knot_hit, resid, 0.0).astype(BF16)
        slot_side = jnp.where(slot_hit, resid, 0.0).astype(BF16)
        knot_term = bf_dot(knot_side, jk, NN)
        land_term = bf_dot(slot_side, jl, NN)
        knot_total = knot_term if knot_total is None else knot_total + knot_term
        land_total = land_term if land_total is None else land_total + land_term

    parted = bf_dot(knot_total.astype(BF16), spread_ref[...], NT).astype(BF16)
    piled = jnp.concatenate(
        [parted[:, i * LANES : (i + 1) * LANES] for i in range(VB)], axis=0
    )
    part = bf_dot(piled, sel_ref[...], TN)[: plan.field]
    part_ref[...] = part.astype(BF16)
    heat = heat + whole_sum(part * knot_dir)
    land_total = land_total.astype(BF16).astype(F32)
    lead_rows = land_total[:, :LANES]
    tail_rows = jnp.concatenate(
        [land_total[:, LANES:], jnp.zeros((plan.slots, LANES - LB), F32)], axis=1
    )
    sums = jnp.zeros((devices, LANES), F32)
    for c in range(cap):
        cut = slice(c * devices, (c + 1) * devices)
        sums = sums + lead_rows[cut] * slot_dir[c] + tail_rows[cut] * slot_dir[cap + c]
    heat = heat + whole_sum(sums)
    high, mid, low = [piece.astype(F32) for piece in split3(heat)]
    if 2 * cap < plan.zrows:
        wide_ref[...] = jnp.zeros_like(wide_ref)
    for c in range(cap):
        cut = slice(c * devices, (c + 1) * devices)
        tail = tail_rows[cut]
        if c == 0:
            tail = jnp.where(lane == LB, high, tail)
            tail = jnp.where(lane == LB + 1, mid, tail)
            tail = jnp.where(lane == LB + 2, low, tail)
        wide_ref[pl.ds(c, devices, stride=plan.zrows), :] = lead_rows[cut]
        wide_ref[pl.ds(cap + c, devices, stride=plan.zrows), :] = tail
    send_ref[...] = wide_ref[...].astype(BF16)


def update_kernel(first, last, plan, *refs):
    refs = list(refs)
    place_ref = refs[0]
    refs = refs[1:]
    rho_ref, knot_dir_ref, land_dir_ref, knot_resid_ref, land_resid_ref = refs[:5]
    knot_damp_ref, land_damp_ref, pick_ref = refs[5:8]
    refs = refs[8:]
    if not first:
        knot_step_ref, land_step_ref = refs[:2]
        refs = refs[2:]
    if not last:
        couple_ref, dinv_ref, cuts_ref, pinv_ref = refs[:4]
        refs = refs[4:]
    part_refs, recv_ref = refs[: plan.n_lm], refs[plan.n_lm]
    refs = refs[plan.n_lm + 1 :]
    knot_step_out, land_step_out, knot_resid_out, land_resid_out = refs[:4]
    refs = refs[4:]
    if not last:
        send_ref, zloc_ref, land_z_ref = refs[:3]
        refs = refs[3:]
        wide_ref, item_ref, stage_ref = refs
    else:
        wide_ref, step_tmp, resid_tmp = refs
    cap, devices, pairs = plan.cap, plan.devices, plan.pairs

    wide_ref[...] = recv_ref[...].astype(F32)
    lane = lax.broadcasted_iota(jnp.int32, (devices, LANES), 1)
    heads = [wide_ref[pl.ds(c, devices, stride=plan.zrows), :] for c in range(cap)]
    tails = [wide_ref[pl.ds(cap + c, devices, stride=plan.zrows), :] for c in range(cap)]
    scalars = (lane >= LB) & (lane < LB + 3)
    alpha = rho_ref[0:1, 0:1] / whole_sum(jnp.where(scalars, tails[0], 0.0))
    lead = bf_dot(pick_ref[...], jnp.concatenate(heads, axis=0).astype(BF16), NN)
    tail = bf_dot(pick_ref[...], jnp.concatenate(tails, axis=0).astype(BF16), NN)
    half = lower_half((pairs, LANES))
    even, odd = lead[:pairs], lead[pairs:]
    grads = [
        jnp.where(half, even, roll_half(odd)),
        jnp.where(half, roll_half(even), odd),
        jnp.where(half, tail[:pairs], roll_half(tail[pairs:])),
    ]

    parts = [ref[...].astype(F32) for ref in part_refs]
    while len(parts) > 1:
        parts = [parts[i] + parts[i + 1] for i in range(0, len(parts), 2)]
    knot_dir = knot_dir_ref[...]
    knot_q = parts[0] + knot_damp_ref[...] * knot_dir
    step = alpha * knot_dir
    knot_step_out[...] = step if first else knot_step_ref[...] + step
    knot_resid_out[...] = knot_resid_ref[...] - alpha * knot_q

    step_to, resid_to = (step_tmp, resid_tmp) if last else (land_step_out, land_resid_out)
    land = []
    for a in range(3):
        spot = pl.ds(a * pairs, pairs)
        along = land_dir_ref[spot, :]
        q = grads[a] + land_damp_ref[spot, :] * along
        step = alpha * along
        step_to[spot, :] = step if first else land_step_ref[spot, :] + step
        value = land_resid_ref[spot, :] - alpha * q
        resid_to[spot, :] = value
        land.append(value)
    if last:
        for j in range(pairs):
            cut = pl.ds(j * LANES, LANES)
            land_step_out[:, cut] = step_tmp[pl.ds(j, 3, stride=pairs), :]
            land_resid_out[:, cut] = resid_tmp[pl.ds(j, 3, stride=pairs), :]
        return
    land_z = scale_land(plan, pinv_ref, land)
    energy = jnp.zeros((pairs, LANES), F32)
    for a in range(3):
        land_z_ref[pl.ds(a * pairs, pairs), :] = land_z[a]
        energy = energy + land[a] * land_z[a]
    out, v1, v12, knot_energy, _, _ = local_sweeps(
        plan, knot_resid_out, couple_ref, dinv_ref, cuts_ref, zloc_ref
    )
    scalar = whole_sum(energy) + leader(place_ref) * whole_sum(knot_energy)
    pack_narrow(
        plan, pick_ref, land_z, scalar, [out, v1, v12], place_ref, item_ref, stage_ref, send_ref
    )


class Arrival:
    def __init__(self, ref, copy):
        self.ref, self.copy, self.shape = ref, copy, ref.shape

    def __getitem__(self, index):
        if self.copy is not None:
            self.copy.wait()
            self.copy = None
        return self.ref[index]


def call(kernel, name, outs, args, scratch):
    args = [arg if isinstance(arg, tuple) else (arg, "far") for arg in args]
    outs = [out if len(out) == 3 else out + ("far",) for out in outs]
    count, made = len(args), len(outs)
    moved = [index for index in range(count) if args[index][1] != "here"]
    values = [
        pltpu.with_memory_space_constraint(arg, pltpu.HBM) if where == "far" else arg
        for arg, where in args
    ]

    def body(*refs):
        sources, refs = list(refs[:count]), refs[count:]
        results, refs = refs[:made], refs[made:]
        landed, rest, sems = refs[: len(moved)], refs[len(moved) : -1], refs[-1]
        for spot, index in enumerate(moved):
            copy = pltpu.make_async_copy(sources[index], landed[spot], sems.at[spot])
            copy.start()
            sources[index] = Arrival(landed[spot], copy)
        place = (lax.axis_index("tm"), lax.axis_index("lm"))
        kernel(place, *sources, *results, *rest)
        for index in moved:
            if sources[index].copy is not None:
                sources[index].copy.wait()

    def entry(where):
        space = {"here": pltpu.VMEM, "far": pltpu.HBM, "any": pl.ANY}[where]
        return pl.BlockSpec(memory_space=space)

    def block(shape, where):
        if where == "here":
            return entry(where)
        return pl.BlockSpec(shape, lambda step: (0,) * len(shape))

    return pl.pallas_call(
        body,
        name=name,
        grid=(1,),
        out_shape=[
            (pltpu.VMEM if where == "here" else pltpu.HBM)(shape, dtype)
            for shape, dtype, where in outs
        ],
        in_specs=[entry(where) for _, where in args],
        out_specs=[block(shape, where) for shape, _, where in outs],
        scratch_shapes=[pltpu.VMEM(args[index][0].shape, args[index][0].dtype) for index in moved]
        + scratch
        + [pltpu.SemaphoreType.DMA((len(moved),))],
        compiler_params=pltpu.CompilerParams(vmem_limit_bytes=24 << 20),
    )(*values)


def exchange(blocks, devices):
    rows = blocks.shape[0] // devices
    shaped = blocks.reshape(devices, rows, LANES)
    moved = lax.all_to_all(shaped, AXES, split_axis=0, concat_axis=0, tiled=True)
    return moved.reshape(blocks.shape)


def swap(value, mask):
    count = lax.axis_size("lm")
    return lax.ppermute(value, "lm", [(i, i ^ mask) for i in range(count)])


def on_device(
    knot_right_side,
    land_rhs,
    jac_knot,
    jac_land,
    obs_knot,
    obs_slot,
    obs_count,
    send_list,
    couple,
    knot_dinv,
    cuts,
    land_pinv,
    knot_damp,
    land_damp,
):
    comps, knots, vehicles = knot_right_side.shape
    observed, height, knot_width = jac_knot.shape
    rows = observed * height
    cap = send_list.shape[2]
    n_tm, n_lm = lax.axis_size("tm"), lax.axis_size("lm")
    plan = Plan(
        comps, knots, land_rhs.shape[1], rows, n_tm, n_lm, cap, jac_land.shape[2]
    )
    devices, slots, field, pairs = plan.devices, plan.slots, plan.field, plan.pairs
    square = comps * comps

    resid = knot_right_side.reshape(field, vehicles)
    couple = couple.reshape(square * knots, vehicles)
    dinv = knot_dinv.reshape(square * knots, vehicles)
    knot_damp = knot_damp.reshape(field, vehicles)
    jk = jac_knot.reshape(rows, knot_width)
    jl = jac_land.reshape(rows, jac_land.shape[2])
    listed = jnp.transpose(send_list[0])

    live = jnp.arange(height, dtype=jnp.int32)[None, :] < obs_count[:, None]
    slot = (obs_slot % cap) * devices + obs_slot // cap
    links = jnp.stack(
        [jnp.where(live, obs_knot[:, None], -1), jnp.where(live, slot[:, None], -1)]
    ).reshape(2, rows)

    groups = vehicles // VB
    lane = jnp.arange(vehicles, dtype=jnp.int32)
    ordered = (lane % groups) * VB + lane // groups
    sel = (ordered[:, None] == lane[None, :]).astype(BF16)
    spot = jnp.arange(VB * LANES, dtype=jnp.int32)
    aim = jnp.where(spot % LANES < field, (spot % LANES) * VB + spot // LANES, -1)
    spread = (aim[:, None] == jnp.arange(knot_width, dtype=jnp.int32)[None, :]).astype(BF16)


    send, zloc, land_resid, land_z, damp, pinv, pick = call(
        functools.partial(start_kernel, plan),
        "start",
        [
            ((devices * plan.rw0, LANES), F32),
            ((field, vehicles), F32, "here"),
            ((3 * pairs, LANES), F32, "here"),
            ((3 * pairs, LANES), F32, "here"),
            ((3 * pairs, LANES), F32),
            ((9 * pairs, LANES), F32),
            ((plan.blocks, slots), BF16),
        ],
        [land_rhs, land_damp, land_pinv, listed, cuts, resid, dinv, couple],
        [
            pltpu.VMEM((plan.held0 * n_lm, 8, LANES), F32),
            pltpu.VMEM((up8(comps * plan.held0), LANES), F32),
        ],
    )
    onward, back = call(
        functools.partial(maps_kernel, plan),
        "maps",
        [((square * knots, vehicles), F32)] * 2,
        [couple, cuts, dinv],
        [],
    )
    state = None
    chain = None
    steps = None
    for turn in range(ITERS):
        first, last = turn == 0, turn == ITERS - 1
        recv = exchange(send, devices)
        args = [(recv, "any" if first else "here")]
        if not first:
            rho, knot_dir, land_dir, slot_dir = state
            args += [(chain, "here"), rho]
            args += [(value, "here") for value in (slot_dir, land_dir, knot_dir)]
        args += [(land_z, "here"), damp, (zloc, "here"), onward, back, knot_damp, sel, spread, links, jl, (jk, "here")]
        outs = [
            ((devices * plan.zrows, LANES), BF16),
            ((field, vehicles), BF16),
            ((8, LANES), F32),
            ((field, vehicles), F32, "here"),
            ((3 * pairs, LANES), F32, "here"),
            ((2 * slots, LANES), F32, "here"),
        ]
        if first:
            outs.append(((n_tm * 2 * square, vehicles), F32, "here"))
        results = call(
            functools.partial(product_kernel, first, plan),
            "product_first" if first else "product",
            outs,
            args,
            [
                pltpu.VMEM((n_tm, 8, vehicles), F32),
                pltpu.VMEM((n_tm, 8, vehicles), F32),
                pltpu.VMEM((devices * plan.zrows, LANES), F32),
            ]
            + (
                []
                if first
                else [
                    pltpu.VMEM((devices * plan.rw, LANES), F32),
                    pltpu.VMEM((devices * plan.per, LANES), F32),
                ]
            ),
        )
        send, part = results[:2]
        state = results[2:6]
        if first:
            chain = results[6]
        rho, knot_dir, land_dir, _ = state
        parts = [part] + [swap(part, mask) for mask in range(1, n_lm)]
        recv = exchange(send, devices)
        args = [rho, (knot_dir, "here"), (land_dir, "here")]
        args += [(resid, "far" if first else "here"), (land_resid, "here"), knot_damp, damp, pick]
        if not first:
            args += [(value, "here") for value in steps]
        wide = pltpu.VMEM((devices * plan.zrows, LANES), F32)
        if not last:
            args += [couple, dinv, cuts, pinv]
        args += parts[:1] + [(value, "here") for value in parts[1:] + [recv]]
        if last:
            outs = [((field, vehicles), F32), ((3, plan.land), F32)] * 2
            scratch = [wide] + [pltpu.VMEM((3 * pairs, LANES), F32)] * 2
        else:
            outs = [((field, vehicles), F32, "here"), ((3 * pairs, LANES), F32, "here")] * 2
            outs += [
                ((devices * plan.rw, LANES), BF16),
                ((field, vehicles), F32, "here"),
                ((3 * pairs, LANES), F32, "here"),
            ]
            scratch = [
                wide,
                pltpu.VMEM((n_lm, up8(plan.per), LANES), F32),
                pltpu.VMEM((devices * plan.rw, LANES), F32),
            ]
        results = call(
            functools.partial(update_kernel, first, last, plan),
            "update_last" if last else "update",
            outs,
            args,
            scratch,
        )
        steps = results[:2]
        resid, land_resid = results[2:4]
        if not last:
            send, zloc, land_z = results[4:]
    shape = (comps, knots, vehicles)
    return (steps[0].reshape(shape), steps[1], resid.reshape(shape), land_resid)


def solution(mesh):
    return jax.shard_map(
        on_device,
        mesh=mesh,
        in_specs=(
            P(None, "tm", None),
            P(None, ("tm", "lm")),
            P(("tm", "lm"), None, None),
            P(("tm", "lm"), None, None),
            P(("tm", "lm")),
            P(("tm", "lm")),
            P(("tm", "lm")),
            P(("tm", "lm"), None, None),
            P(None, None, "tm", None),
            P(None, None, "tm", None),
            P("tm", None),
            P(None, None, ("tm", "lm")),
            P(None, "tm", None),
            P(None, ("tm", "lm")),
        ),
        out_specs=(
            P(None, "tm", None),
            P(None, ("tm", "lm")),
            P(None, "tm", None),
            P(None, ("tm", "lm")),
        ),
        check_vma=False,
    )
```

```python
import functools
import jax
import jax.numpy as jnp
from jax import lax
from jax.experimental import pallas as pl
from jax.experimental.pallas import tpu as pltpu
from jax.sharding import PartitionSpec as P

VB = 4
LB = 64
ITERS = 3
LANES = 128
AXES = ("tm", "lm")
F32 = jnp.float32
BF16 = jnp.bfloat16

NT = (((1,), (1,)), ((), ()))
TN = (((0,), (0,)), ((), ()))
NN = (((1,), (0,)), ((), ()))


def up8(value):
    return (value + 7) // 8 * 8


def bf_dot(left, right, dims):
    return lax.dot_general(left, right, dims, preferred_element_type=F32)


def matvec(tiles, vector):
    total = tiles[0] * vector[0:1]
    for index in range(1, len(tiles)):
        total = total + tiles[index] * vector[index : index + 1]
    return total


def whole_sum(value):
    return jnp.sum(jnp.sum(value, axis=0, keepdims=True), axis=1, keepdims=True)


class Plan:
    def __init__(self, comps, knots, land, rows, n_tm, n_lm, cap, width):
        self.comps, self.knots, self.land, self.rows = comps, knots, land, rows
        self.n_tm, self.n_lm, self.cap = n_tm, n_lm, cap
        self.devices = n_tm * n_lm
        self.slots = self.devices * cap
        self.width = width
        self.field = comps * knots
        self.pairs = land // LANES
        self.blocks = land // LB
        self.zrows = up8(2 * cap)
        self.items0 = 5 + 4 * comps
        self.held0 = -(-self.items0 // n_lm)
        self.rw0 = self.zrows + up8(comps * self.held0)
        self.per = -(-5 * comps // n_lm)
        self.rw = self.zrows + up8(self.per)

    def item_row(self, source, item):
        holder = source * self.n_lm + item % self.n_lm
        return holder * self.rw0 + self.zrows + self.comps * (item // self.n_lm)


def col_tiles(ref, plan, k):
    step = plan.comps * plan.knots
    return [
        ref[pl.ds(b * plan.knots + k, plan.comps, stride=step), :] for b in range(plan.comps)
    ]


def row_tiles(ref, plan, k):
    step = plan.comps * plan.knots
    return [
        ref[pl.ds(a * step + k, plan.comps, stride=plan.knots), :] for a in range(plan.comps)
    ]


def local_sweeps(plan, resid_ref, couple_ref, dinv_ref, cuts_ref, zloc_ref, maps=False):
    comps, knots = plan.comps, plan.knots
    lanes = couple_ref.shape[1]
    minus = cuts_ref[...].astype(F32) - 1.0
    carry = None
    basis = []
    if maps:
        rows = lax.broadcasted_iota(jnp.int32, (comps, lanes), 0)
        basis = [(rows == b).astype(F32) for b in range(comps)]
    scaled, turned, scaled_maps = [], [], []
    energy = jnp.zeros((comps, lanes), F32)
    for k in range(knots):
        value = resid_ref[pl.ds(k, comps, stride=knots), :]
        if carry is not None:
            value = value + carry
        dcol = col_tiles(dinv_ref, plan, k)
        y = matvec(dcol, value)
        scaled.append(y)
        turned.append(matvec(row_tiles(dinv_ref, plan, k), value))
        energy = energy + value * y
        lcol = col_tiles(couple_ref, plan, k)
        gate = minus[k : k + 1]
        carry = gate * matvec(lcol, value)
        if maps:
            scaled_maps.append([matvec(dcol, col) for col in basis])
            basis = [gate * matvec(lcol, col) for col in basis]
    out = carry
    total = basis
    z, u = None, None
    onward = [None] * comps
    for k in reversed(range(knots)):
        lrow = row_tiles(couple_ref, plan, k)
        gate = minus[k : k + 1]
        z = scaled[k] if z is None else scaled[k] + gate * matvec(lrow, z)
        u = turned[k] if u is None else turned[k] + gate * matvec(lrow, u)
        zloc_ref[pl.ds(k, comps, stride=knots), :] = z
        if maps:
            onward = [
                scaled_maps[k][b]
                if onward[b] is None
                else scaled_maps[k][b] + gate * matvec(lrow, onward[b])
                for b in range(comps)
            ]
    return out, z, z + u, energy, total, onward


def maps_kernel(plan, place_ref, couple_ref, cuts_ref, dinv_ref, onward_ref, back_ref):
    comps, knots = plan.comps, plan.knots
    minus = cuts_ref[...].astype(F32) - 1.0
    rows = lax.broadcasted_iota(jnp.int32, (comps, couple_ref.shape[1]), 0)
    eye = [(rows == b).astype(F32) for b in range(comps)]
    basis, scaled = eye, []
    for k in range(knots):
        dcol = col_tiles(dinv_ref, plan, k)
        scaled.append([matvec(dcol, col) for col in basis])
        if k + 1 < knots:
            lcol = col_tiles(couple_ref, plan, k)
            basis = [minus[k : k + 1] * matvec(lcol, col) for col in basis]
    onward, back = None, eye
    for k in reversed(range(knots)):
        lrow = row_tiles(couple_ref, plan, k)
        gate = minus[k : k + 1]
        back = [gate * matvec(lrow, col) for col in back]
        if onward is None:
            onward = scaled[k]
        else:
            onward = [scaled[k][b] + gate * matvec(lrow, onward[b]) for b in range(comps)]
        for b in range(comps):
            spot = pl.ds(b * knots + k, comps, stride=comps * knots)
            onward_ref[spot, :] = onward[b]
            back_ref[spot, :] = back[b]


def scale_land(plan, pinv_ref, land):
    pairs = plan.pairs
    result = []
    for a in range(3):
        total = pinv_ref[pl.ds(3 * a * pairs, pairs), :] * land[0]
        for b in range(1, 3):
            total = total + pinv_ref[pl.ds((3 * a + b) * pairs, pairs), :] * land[b]
        result.append(total)
    return result


def lower_half(shape):
    return lax.broadcasted_iota(jnp.int32, shape, 1) < LB


def roll_half(value):
    return pltpu.roll(value, LB, 1)


def split3(value):
    high = value.astype(BF16)
    rest = value - high.astype(F32)
    mid = rest.astype(BF16)
    low = (rest - mid.astype(F32)).astype(BF16)
    return high, mid, low


def land_blocks(land_z):
    half = lower_half(land_z[0].shape)
    z0, z1, z2 = land_z
    r0, r1, r2 = roll_half(z0), roll_half(z1), roll_half(z2)
    zero = jnp.zeros_like(z0)
    first = jnp.concatenate([jnp.where(half, z0, r1), jnp.where(half, r0, z1)], axis=0)
    second = jnp.concatenate([jnp.where(half, z2, zero), jnp.where(half, r2, zero)], axis=0)
    return jnp.concatenate([first, second], axis=1)


def place_land(plan, rw, rows, marks, stage_ref):
    devices, cap = plan.devices, plan.cap
    lane = lax.broadcasted_iota(jnp.int32, (devices, LANES), 1)
    for c in range(cap):
        part = rows[c * devices : (c + 1) * devices]
        tail = part[:, LANES:]
        if c == 0:
            for index, mark in enumerate(marks):
                tail = jnp.where(lane == LB + index, mark, tail)
        stage_ref[pl.ds(c, devices, stride=rw), :] = part[:, :LANES]
        stage_ref[pl.ds(cap + c, devices, stride=rw), :] = tail
    for unused in range(2 * cap, plan.zrows):
        stage_ref[pl.ds(unused, devices, stride=rw), :] = jnp.zeros((devices, LANES), F32)


def in_pieces(items, alone):
    pieces = []
    for index, item in enumerate(items):
        if index in alone:
            pieces.append(item)
        else:
            high, low, _ = split3(item)
            pieces += [high.astype(F32), low.astype(F32)]
    return pieces


def pack_start(plan, pick_ref, land_z, scalar, items, place_ref, item_ref, tile_ref, stage_ref, send_ref):
    rw, comps = plan.rw0, plan.comps
    rows = bf_dot(pick_ref[...], land_blocks(land_z).astype(BF16), TN)
    place_land(plan, rw, rows, [piece.astype(F32) for piece in split3(scalar)], stage_ref)
    item_ref[...] = jnp.zeros_like(item_ref)
    for index, piece in enumerate(in_pieces(items, (2,))):
        item_ref[index, pl.ds(0, comps), :] = piece
    tile_ref[...] = jnp.zeros_like(tile_ref)
    mine = place_ref[1]
    for k in range(plan.held0):
        tile_ref[pl.ds(comps * k, comps), :] = item_ref[k * plan.n_lm + mine, pl.ds(0, comps), :]
    tile = tile_ref[...]
    for d in range(plan.devices):
        stage_ref[pl.ds(d * rw + plan.zrows, rw - plan.zrows), :] = tile
    send_ref[...] = stage_ref[...].astype(BF16)


def pack_narrow(plan, pick_ref, land_z, scalar, items, place_ref, item_ref, stage_ref, send_ref):
    rw, comps, per = plan.rw, plan.comps, plan.per
    rows = bf_dot(pick_ref[...], land_blocks(land_z).astype(BF16), TN)
    place_land(plan, rw, rows, [piece.astype(F32) for piece in split3(scalar)], stage_ref)
    pieces = in_pieces(items, (2,))
    item_ref[...] = jnp.zeros_like(item_ref)
    for index, piece in enumerate(pieces):
        begin = 0
        while begin < comps:
            flat = comps * index + begin
            run = min(comps - begin, per - flat % per)
            item_ref[flat // per, pl.ds(flat % per, run), :] = piece[begin : begin + run]
            begin += run
    tile = item_ref[place_ref[1]]
    for d in range(plan.devices):
        stage_ref[pl.ds(d * rw + plan.zrows, rw - plan.zrows), :] = tile
    send_ref[...] = stage_ref[...].astype(BF16)


def leader(place_ref):
    return (place_ref[1] == 0).astype(F32)


def start_kernel(
    plan,
    place_ref,
    rhs_ref,
    damp_ref,
    pinv_ref,
    list_ref,
    cuts_ref,
    resid_ref,
    dinv_ref,
    couple_ref,
    send_ref,
    zloc_ref,
    land_ref,
    land_z_ref,
    land_damp_ref,
    land_pinv_ref,
    pick_ref,
    item_ref,
    tile_ref,
    stage_ref,
):
    pairs = plan.pairs
    for j in range(pairs):
        cut = pl.ds(j * LANES, LANES)
        land_ref[pl.ds(j, 3, stride=pairs), :] = rhs_ref[:, cut]
        land_damp_ref[pl.ds(j, 3, stride=pairs), :] = damp_ref[:, cut]
        for a in range(3):
            land_pinv_ref[pl.ds(3 * a * pairs + j, 3, stride=pairs), :] = pinv_ref[a, :, cut]
    index = lax.broadcasted_iota(jnp.int32, (plan.blocks, plan.slots), 0)
    wanted = list_ref[...]
    wanted = jnp.concatenate([wanted[c : c + 1] for c in range(plan.cap)], axis=1)
    wanted = (wanted % 2) * pairs + wanted // 2
    pick_ref[...] = (index == wanted).astype(F32).astype(BF16)
    land = [land_ref[pl.ds(a * pairs, pairs), :] for a in range(3)]
    land_z = scale_land(plan, land_pinv_ref, land)
    energy = jnp.zeros((pairs, LANES), F32)
    for a in range(3):
        land_z_ref[pl.ds(a * pairs, pairs), :] = land_z[a]
        energy = energy + land[a] * land_z[a]
    out, v1, v12, knot_energy, total, inner = local_sweeps(
        plan, resid_ref, couple_ref, dinv_ref, cuts_ref, zloc_ref, True
    )
    scalar = whole_sum(energy) + leader(place_ref) * whole_sum(knot_energy)
    pack_start(
        plan, pick_ref, land_z, scalar, [out, v1, v12] + total + inner,
        place_ref, item_ref, tile_ref, stage_ref, send_ref,
    )


def product_kernel(first, plan, *refs):
    refs = list(refs)
    place_ref, recv_ref = refs[:2]
    refs = refs[2:]
    rw = plan.rw0 if first else plan.rw
    if not first:
        chain_in_ref, rho_in_ref, slot_in_ref, land_in_ref, knot_in_ref = refs[:5]
        refs = refs[5:]
    land_z_ref, land_damp_ref, zloc_ref, onward_ref, back_ref = refs[:5]
    knot_damp_ref, sel_ref, link_ref, jl_ref, jk_ref = refs[5:10]
    outs = refs[10:]
    send_ref, part_ref, rho_ref, knot_ref, land_ref, slot_ref = outs[:6]
    outs = outs[6:]
    if first:
        chain_ref = outs[0]
        outs = outs[1:]
    else:
        chain_ref = chain_in_ref
    entry_ref, arrive_ref, wide_ref = outs[:3]
    outs = outs[3:]
    comps, knots, cap, devices = plan.comps, plan.knots, plan.cap, plan.devices
    lanes = zloc_ref.shape[1]
    square = comps * comps

    got_ref = outs[0]
    got_ref[...] = recv_ref[...].astype(F32)
    recv_ref = got_ref
    if first:

        def piece(s, index):
            return got_ref[pl.ds(plan.item_row(s, index), comps), :]

        def item(s, index):
            if index == 2:
                return piece(s, 4)
            spot = 2 * index if index < 2 else 2 * index - 1
            return piece(s, spot) + piece(s, spot + 1)

        for s in range(plan.n_tm):
            for m in range(2 * comps):
                chain_ref[pl.ds(s * 2 * square + m * comps, comps), :] = item(s, 3 + m)

    else:
        flat_ref = outs[1]
        per = plan.per
        for d in range(devices):
            flat_ref[pl.ds(d * per, per), :] = got_ref[pl.ds(d * rw + plan.zrows, per), :]

        def item(s, index):
            base = s * plan.n_lm * per
            if index == 2:
                return flat_ref[pl.ds(base + 4 * comps, comps), :]
            begin = base + 2 * index * comps
            high = flat_ref[pl.ds(begin, comps), :]
            return high + flat_ref[pl.ds(begin + comps, comps), :]

    incoming = None
    firsts = []
    heat = jnp.zeros((comps, lanes), F32)
    for s in range(plan.n_tm):
        base = s * 2 * square
        v1 = item(s, 1)
        if incoming is None:
            entry_ref[s, pl.ds(0, comps), :] = jnp.zeros((comps, lanes), F32)
            firsts.append(v1)
            incoming = item(s, 0)
        else:
            entry_ref[s, pl.ds(0, comps), :] = incoming
            inner = [chain_ref[pl.ds(base + square + b * comps, comps), :] for b in range(comps)]
            pushed = matvec(inner, incoming)
            heat = heat + incoming * (item(s, 2) + pushed)
            firsts.append(v1 + pushed)
            if s + 1 < plan.n_tm:
                total = [chain_ref[pl.ds(base + b * comps, comps), :] for b in range(comps)]
                incoming = matvec(total, incoming) + item(s, 0)
    arriving = None
    for s in reversed(range(plan.n_tm)):
        base = s * 2 * square
        if arriving is None:
            arrive_ref[s, pl.ds(0, comps), :] = jnp.zeros((comps, lanes), F32)
            arriving = firsts[s]
        else:
            arrive_ref[s, pl.ds(0, comps), :] = arriving
            if s > 0:
                back = [
                    chain_ref[pl.ds(base + a, comps, stride=comps), :] for a in range(comps)
                ]
                arriving = firsts[s] + matvec(back, arriving)

    lane = lax.broadcasted_iota(jnp.int32, (devices, LANES), 1)
    tails = [recv_ref[pl.ds(cap + c, devices, stride=rw), :] for c in range(cap)]
    heads = [recv_ref[pl.ds(c, devices, stride=rw), :] for c in range(cap)]
    marked = (lane >= LB) & (lane < LB + 3)
    rho = whole_sum(jnp.where(marked, tails[0], 0.0)) + whole_sum(heat)
    rho_ref[...] = jnp.broadcast_to(rho, rho_ref.shape)
    if not first:
        beta = rho / rho_in_ref[0:1, 0:1]
    half = lane < LB
    tails = [jnp.where(half, tail, 0.0) for tail in tails]
    slot_dir = []
    for index, rows in enumerate(heads + tails):
        spot = pl.ds(index * devices, devices)
        if not first:
            rows = rows + beta * slot_in_ref[spot, :]
        slot_ref[spot, :] = rows
        slot_dir.append(rows)
    land_dir = land_z_ref[...]
    if not first:
        land_dir = land_dir + beta * land_in_ref[...]
    land_ref[...] = land_dir
    heat = whole_sum(land_damp_ref[...] * land_dir * land_dir)

    mine = place_ref[0]
    entry = entry_ref[mine, pl.ds(0, comps), :]
    arrive = arrive_ref[mine, pl.ds(0, comps), :]
    for a in range(comps):
        total = zloc_ref[pl.ds(a * knots, knots), :]
        for b in range(comps):
            spot = pl.ds((a * comps + b) * knots, knots)
            total = total + onward_ref[spot, :] * entry[b : b + 1]
            total = total + back_ref[spot, :] * arrive[b : b + 1]
        if not first:
            total = total + beta * knot_in_ref[pl.ds(a * knots, knots), :]
        knot_ref[pl.ds(a * knots, knots), :] = total
    knot_dir = knot_ref[...]
    heat = heat + leader(place_ref) * whole_sum(knot_damp_ref[...] * knot_dir * knot_dir)

    groups = lanes // VB
    turned = bf_dot(sel_ref[...], knot_dir.astype(BF16), NT)
    knot_rows = jnp.concatenate(
        [turned[i * groups : (i + 1) * groups] for i in range(VB)], axis=1
    ).astype(BF16)
    slot_rows = jnp.concatenate(
        [
            jnp.concatenate(slot_dir[:cap], axis=0).astype(BF16),
            jnp.concatenate(slot_dir[cap:], axis=0).astype(BF16)[:, :LB],
        ],
        axis=1,
    )
    chunk = plan.rows // 3 if plan.rows % (3 * LANES) == 0 else plan.rows
    knot_total, land_total = None, None

    def ahead(start):
        cut = pl.ds(start, chunk)
        near = bf_dot(knot_rows, jk_ref[cut, :], NT)
        return near, bf_dot(slot_rows, jl_ref[cut, :], NT)

    ready = ahead(0)
    for start in range(0, plan.rows, chunk):
        near, far = ready
        if start + chunk < plan.rows:
            ready = ahead(start + chunk)
        cut = pl.ds(start, chunk)
        knot_hit = lax.broadcasted_iota(jnp.int32, near.shape, 0) == link_ref[0:1, cut]
        slot_hit = lax.broadcasted_iota(jnp.int32, far.shape, 0) == link_ref[1:2, cut]
        resid = jnp.sum(jnp.where(knot_hit, near, 0.0), axis=0, keepdims=True) + jnp.sum(
            jnp.where(slot_hit, far, 0.0), axis=0, keepdims=True
        )
        knot_side = jnp.where(knot_hit, resid, 0.0).astype(BF16)
        slot_side = jnp.where(slot_hit, resid, 0.0).astype(BF16)
        knot_term = bf_dot(knot_side, jk_ref[cut, :], NN)
        land_term = bf_dot(slot_side, jl_ref[cut, :], NN)
        knot_total = knot_term if knot_total is None else knot_total + knot_term
        land_total = land_term if land_total is None else land_total + land_term

    piled = jnp.concatenate(
        [knot_total[:, i * plan.field : (i + 1) * plan.field] for i in range(VB)], axis=0
    ).astype(BF16)
    part = bf_dot(piled, sel_ref[...], TN)
    part_ref[...] = part.astype(BF16)
    heat = heat + whole_sum(part * knot_dir)
    land_total = land_total.astype(BF16).astype(F32)
    lead_rows = land_total[:, :LANES]
    tail_rows = jnp.concatenate(
        [land_total[:, LANES:], jnp.zeros((plan.slots, LANES - LB), F32)], axis=1
    )
    sums = jnp.zeros((devices, LANES), F32)
    for c in range(cap):
        cut = slice(c * devices, (c + 1) * devices)
        sums = sums + lead_rows[cut] * slot_dir[c] + tail_rows[cut] * slot_dir[cap + c]
    heat = heat + whole_sum(sums)
    high, mid, low = [piece.astype(F32) for piece in split3(heat)]
    if 2 * cap < plan.zrows:
        wide_ref[...] = jnp.zeros_like(wide_ref)
    for c in range(cap):
        cut = slice(c * devices, (c + 1) * devices)
        tail = tail_rows[cut]
        if c == 0:
            tail = jnp.where(lane == LB, high, tail)
            tail = jnp.where(lane == LB + 1, mid, tail)
            tail = jnp.where(lane == LB + 2, low, tail)
        wide_ref[pl.ds(c, devices, stride=plan.zrows), :] = lead_rows[cut]
        wide_ref[pl.ds(cap + c, devices, stride=plan.zrows), :] = tail
    send_ref[...] = wide_ref[...].astype(BF16)


def order_kernel(plan, place_ref, order_ref, jk_ref, out_ref):
    chunk = 512
    for start in range(0, plan.rows, chunk):
        cut = pl.ds(start, chunk)
        out_ref[cut, :] = bf_dot(jk_ref[cut, :], order_ref[...], NT).astype(BF16)


def update_kernel(first, last, plan, *refs):
    refs = list(refs)
    place_ref = refs[0]
    refs = refs[1:]
    rho_ref, knot_dir_ref, land_dir_ref, knot_resid_ref, land_resid_ref = refs[:5]
    knot_damp_ref, land_damp_ref, pick_ref = refs[5:8]
    refs = refs[8:]
    if not first:
        knot_step_ref, land_step_ref = refs[:2]
        refs = refs[2:]
    if not last:
        couple_ref, dinv_ref, cuts_ref, pinv_ref = refs[:4]
        refs = refs[4:]
    part_refs, recv_ref = refs[: plan.n_lm], refs[plan.n_lm]
    refs = refs[plan.n_lm + 1 :]
    knot_step_out, land_step_out, knot_resid_out, land_resid_out = refs[:4]
    refs = refs[4:]
    if not last:
        send_ref, zloc_ref, land_z_ref = refs[:3]
        refs = refs[3:]
        wide_ref, item_ref, stage_ref = refs
    else:
        wide_ref, step_tmp, resid_tmp = refs
    cap, devices, pairs = plan.cap, plan.devices, plan.pairs

    wide_ref[...] = recv_ref[...].astype(F32)
    lane = lax.broadcasted_iota(jnp.int32, (devices, LANES), 1)
    heads = [wide_ref[pl.ds(c, devices, stride=plan.zrows), :] for c in range(cap)]
    tails = [wide_ref[pl.ds(cap + c, devices, stride=plan.zrows), :] for c in range(cap)]
    scalars = (lane >= LB) & (lane < LB + 3)
    alpha = rho_ref[0:1, 0:1] / whole_sum(jnp.where(scalars, tails[0], 0.0))
    lead = bf_dot(pick_ref[...], jnp.concatenate(heads, axis=0).astype(BF16), NN)
    tail = bf_dot(pick_ref[...], jnp.concatenate(tails, axis=0).astype(BF16), NN)
    half = lower_half((pairs, LANES))
    even, odd = lead[:pairs], lead[pairs:]
    grads = [
        jnp.where(half, even, roll_half(odd)),
        jnp.where(half, roll_half(even), odd),
        jnp.where(half, tail[:pairs], roll_half(tail[pairs:])),
    ]

    parts = [ref[...].astype(F32) for ref in part_refs]
    while len(parts) > 1:
        parts = [parts[i] + parts[i + 1] for i in range(0, len(parts), 2)]
    knot_dir = knot_dir_ref[...]
    knot_q = parts[0] + knot_damp_ref[...] * knot_dir
    step = alpha * knot_dir
    knot_step_out[...] = step if first else knot_step_ref[...] + step
    knot_resid_out[...] = knot_resid_ref[...] - alpha * knot_q

    step_to, resid_to = (step_tmp, resid_tmp) if last else (land_step_out, land_resid_out)
    land = []
    for a in range(3):
        spot = pl.ds(a * pairs, pairs)
        along = land_dir_ref[spot, :]
        q = grads[a] + land_damp_ref[spot, :] * along
        step = alpha * along
        step_to[spot, :] = step if first else land_step_ref[spot, :] + step
        value = land_resid_ref[spot, :] - alpha * q
        resid_to[spot, :] = value
        land.append(value)
    if last:
        for j in range(pairs):
            cut = pl.ds(j * LANES, LANES)
            land_step_out[:, cut] = step_tmp[pl.ds(j, 3, stride=pairs), :]
            land_resid_out[:, cut] = resid_tmp[pl.ds(j, 3, stride=pairs), :]
        return
    land_z = scale_land(plan, pinv_ref, land)
    energy = jnp.zeros((pairs, LANES), F32)
    for a in range(3):
        land_z_ref[pl.ds(a * pairs, pairs), :] = land_z[a]
        energy = energy + land[a] * land_z[a]
    out, v1, v12, knot_energy, _, _ = local_sweeps(
        plan, knot_resid_out, couple_ref, dinv_ref, cuts_ref, zloc_ref
    )
    scalar = whole_sum(energy) + leader(place_ref) * whole_sum(knot_energy)
    pack_narrow(
        plan, pick_ref, land_z, scalar, [out, v1, v12], place_ref, item_ref, stage_ref, send_ref
    )


class Arrival:
    def __init__(self, ref, copy):
        self.ref, self.copy, self.shape = ref, copy, ref.shape

    def __getitem__(self, index):
        if self.copy is not None:
            self.copy.wait()
            self.copy = None
        return self.ref[index]


def call(kernel, name, outs, args, scratch):
    args = [arg if isinstance(arg, tuple) else (arg, "far") for arg in args]
    outs = [out if len(out) == 3 else out + ("far",) for out in outs]
    count, made = len(args), len(outs)
    moved = [index for index in range(count) if args[index][1] != "here"]
    values = [
        pltpu.with_memory_space_constraint(arg, pltpu.HBM) if where == "far" else arg
        for arg, where in args
    ]

    def body(*refs):
        sources, refs = list(refs[:count]), refs[count:]
        results, refs = refs[:made], refs[made:]
        landed, rest, sems = refs[: len(moved)], refs[len(moved) : -1], refs[-1]
        for spot, index in enumerate(moved):
            copy = pltpu.make_async_copy(sources[index], landed[spot], sems.at[spot])
            copy.start()
            sources[index] = Arrival(landed[spot], copy)
        place = (lax.axis_index("tm"), lax.axis_index("lm"))
        kernel(place, *sources, *results, *rest)
        for index in moved:
            if sources[index].copy is not None:
                sources[index].copy.wait()

    def entry(where):
        space = {"here": pltpu.VMEM, "far": pltpu.HBM, "any": pl.ANY}[where]
        return pl.BlockSpec(memory_space=space)

    def block(shape, where):
        if where == "here":
            return entry(where)
        return pl.BlockSpec(shape, lambda step: (0,) * len(shape))

    return pl.pallas_call(
        body,
        name=name,
        grid=(1,),
        out_shape=[
            (pltpu.VMEM if where == "here" else pltpu.HBM)(shape, dtype)
            for shape, dtype, where in outs
        ],
        in_specs=[entry(where) for _, where in args],
        out_specs=[block(shape, where) for shape, _, where in outs],
        scratch_shapes=[pltpu.VMEM(args[index][0].shape, args[index][0].dtype) for index in moved]
        + scratch
        + [pltpu.SemaphoreType.DMA((len(moved),))],
        compiler_params=pltpu.CompilerParams(vmem_limit_bytes=24 << 20),
    )(*values)


def exchange(blocks, devices):
    rows = blocks.shape[0] // devices
    shaped = blocks.reshape(devices, rows, LANES)
    moved = lax.all_to_all(shaped, AXES, split_axis=0, concat_axis=0, tiled=True)
    return moved.reshape(blocks.shape)


def swap(value, mask):
    count = lax.axis_size("lm")
    return lax.ppermute(value, "lm", [(i, i ^ mask) for i in range(count)])


def on_device(
    knot_right_side,
    land_rhs,
    jac_knot,
    jac_land,
    obs_knot,
    obs_slot,
    obs_count,
    send_list,
    couple,
    knot_dinv,
    cuts,
    land_pinv,
    knot_damp,
    land_damp,
):
    comps, knots, vehicles = knot_right_side.shape
    observed, height, knot_width = jac_knot.shape
    rows = observed * height
    cap = send_list.shape[2]
    n_tm, n_lm = lax.axis_size("tm"), lax.axis_size("lm")
    plan = Plan(
        comps, knots, land_rhs.shape[1], rows, n_tm, n_lm, cap, jac_land.shape[2]
    )
    devices, slots, field, pairs = plan.devices, plan.slots, plan.field, plan.pairs
    square = comps * comps

    resid = knot_right_side.reshape(field, vehicles)
    couple = couple.reshape(square * knots, vehicles)
    dinv = knot_dinv.reshape(square * knots, vehicles)
    knot_damp = knot_damp.reshape(field, vehicles)
    jk = jac_knot.reshape(rows, knot_width)
    jl = jac_land.reshape(rows, jac_land.shape[2])
    listed = jnp.transpose(send_list[0])

    live = jnp.arange(height, dtype=jnp.int32)[None, :] < obs_count[:, None]
    slot = (obs_slot % cap) * devices + obs_slot // cap
    links = jnp.stack(
        [jnp.where(live, obs_knot[:, None], -1), jnp.where(live, slot[:, None], -1)]
    ).reshape(2, rows)

    groups = vehicles // VB
    lane = jnp.arange(vehicles, dtype=jnp.int32)
    ordered = (lane % groups) * VB + lane // groups
    sel = (ordered[:, None] == lane[None, :]).astype(BF16)
    spot = jnp.arange(knot_width, dtype=jnp.int32)
    aim = (spot % field) * VB + spot // field
    order = (aim[:, None] == spot[None, :]).astype(BF16)

    send, zloc, land_resid, land_z, damp, pinv, pick = call(
        functools.partial(start_kernel, plan),
        "start",
        [
            ((devices * plan.rw0, LANES), BF16),
            ((field, vehicles), F32, "here"),
            ((3 * pairs, LANES), F32, "here"),
            ((3 * pairs, LANES), F32, "here"),
            ((3 * pairs, LANES), F32),
            ((9 * pairs, LANES), F32),
            ((plan.blocks, slots), BF16),
        ],
        [land_rhs, land_damp, land_pinv, listed, cuts, resid, dinv, couple],
        [
            pltpu.VMEM((plan.held0 * n_lm, 8, LANES), F32),
            pltpu.VMEM((up8(comps * plan.held0), LANES), F32),
            pltpu.VMEM((devices * plan.rw0, LANES), F32),
        ],
    )
    onward, back = call(
        functools.partial(maps_kernel, plan),
        "maps",
        [((square * knots, vehicles), F32)] * 2,
        [couple, cuts, dinv],
        [],
    )
    (jk,) = call(
        functools.partial(order_kernel, plan),
        "order",
        [((rows, knot_width), BF16, "here")],
        [order, jk],
        [],
    )
    state = None
    chain = None
    steps = None
    for turn in range(ITERS):
        first, last = turn == 0, turn == ITERS - 1
        recv = exchange(send, devices)
        args = [(recv, "any" if first else "here")]
        if not first:
            rho, knot_dir, land_dir, slot_dir = state
            args += [(chain, "here"), rho]
            args += [(value, "here") for value in (slot_dir, land_dir, knot_dir)]
        args += [(land_z, "here"), damp, (zloc, "here"), onward, back, knot_damp, sel, links, jl, (jk, "here")]
        outs = [
            ((devices * plan.zrows, LANES), BF16),
            ((field, vehicles), BF16),
            ((8, LANES), F32),
            ((field, vehicles), F32, "here"),
            ((3 * pairs, LANES), F32, "here"),
            ((2 * slots, LANES), F32, "here"),
        ]
        if first:
            outs.append(((n_tm * 2 * square, vehicles), F32, "here"))
        results = call(
            functools.partial(product_kernel, first, plan),
            "product_first" if first else "product",
            outs,
            args,
            [
                pltpu.VMEM((n_tm, 8, vehicles), F32),
                pltpu.VMEM((n_tm, 8, vehicles), F32),
                pltpu.VMEM((devices * plan.zrows, LANES), F32),
            ]
            + [
                pltpu.VMEM((devices * (plan.rw0 if first else plan.rw), LANES), F32),
                pltpu.VMEM((devices * plan.per, LANES), F32),
            ],
        )
        send, part = results[:2]
        state = results[2:6]
        if first:
            chain = results[6]
        rho, knot_dir, land_dir, _ = state
        parts = [part] + [swap(part, mask) for mask in range(1, n_lm)]
        recv = exchange(send, devices)
        args = [rho, (knot_dir, "here"), (land_dir, "here")]
        args += [(resid, "far" if first else "here"), (land_resid, "here"), knot_damp, damp, pick]
        if not first:
            args += [(value, "here") for value in steps]
        wide = pltpu.VMEM((devices * plan.zrows, LANES), F32)
        if not last:
            args += [couple, dinv, cuts, pinv]
        args += parts[:1] + [(value, "here") for value in parts[1:] + [recv]]
        if last:
            outs = [((field, vehicles), F32), ((3, plan.land), F32)] * 2
            scratch = [wide] + [pltpu.VMEM((3 * pairs, LANES), F32)] * 2
        else:
            outs = [((field, vehicles), F32, "here"), ((3 * pairs, LANES), F32, "here")] * 2
            outs += [
                ((devices * plan.rw, LANES), BF16),
                ((field, vehicles), F32, "here"),
                ((3 * pairs, LANES), F32, "here"),
            ]
            scratch = [
                wide,
                pltpu.VMEM((n_lm, up8(plan.per), LANES), F32),
                pltpu.VMEM((devices * plan.rw, LANES), F32),
            ]
        results = call(
            functools.partial(update_kernel, first, last, plan),
            "update_last" if last else "update",
            outs,
            args,
            scratch,
        )
        steps = results[:2]
        resid, land_resid = results[2:4]
        if not last:
            send, zloc, land_z = results[4:]
    shape = (comps, knots, vehicles)
    return (steps[0].reshape(shape), steps[1], resid.reshape(shape), land_resid)


def solution(mesh):
    return jax.shard_map(
        on_device,
        mesh=mesh,
        in_specs=(
            P(None, "tm", None),
            P(None, ("tm", "lm")),
            P(("tm", "lm"), None, None),
            P(("tm", "lm"), None, None),
            P(("tm", "lm")),
            P(("tm", "lm")),
            P(("tm", "lm")),
            P(("tm", "lm"), None, None),
            P(None, None, "tm", None),
            P(None, None, "tm", None),
            P("tm", None),
            P(None, None, ("tm", "lm")),
            P(None, "tm", None),
            P(None, ("tm", "lm")),
        ),
        out_specs=(
            P(None, "tm", None),
            P(None, ("tm", "lm")),
            P(None, "tm", None),
            P(None, ("tm", "lm")),
        ),
        check_vma=False,
    )
```
